768 devices in a mesh: grp: 48 (over x, z_lo, core), col: 8 (over y), dev: 2 (over z_hi).
Axes of the slice: x: 4, y: 8, z: 12 (z_hi: 2, z_lo: 6; z = z_hi * 6 + z_lo), core: 2. Of those that a mesh axis runs over, the one named last changes fastest.
Arguments:
- rho_re: float32 [12288, 512], P(('grp', 'col'), 'dev'), may hold values from -0.078125 to 0.078125
- rho_im: float32 [12288, 512], P(('grp', 'col'), 'dev'), may hold values from -0.078125 to 0.078125
- coulomb: float32 [12288], P(('grp', 'col', 'dev')), may hold values from 0.4 to 1.6
- chi_prev: float32 [2, 48, 8, 32, 12288], P(None, None, 'col', 'dev', 'grp'), may hold values from -0.013671875 to 0.013671875
- source: float32 [12288, 128], P(('grp', 'col', 'dev')), may hold values from -6 to 6
- band_v: int32 [512], P('dev'), may hold values from 0 to 127
- band_c: int32 [512], P('dev'), may hold values from 128 to 255
- band_energy: float32 [256], replicated, may hold values from -2 to 2.5, as said below
- band_occ: float32 [256], replicated, may hold values from 0 to 1, as said below
Outputs:
- screened_re: float32 [12288, 128], P(('grp', 'col', 'dev'))
- screened_im: float32 [12288, 128], P(('grp', 'col', 'dev'))
The draws below stay inside these ranges and needn't reach their ends.
Inputs may be any that keep to these rules, and one draw needn't show every extreme that they name: `band_v`: the valence bands are the first 128. `band_energy`: the first 128 bands lie below -0.1, the others above 0.2. `band_occ`: the first 128 bands have occupations of 0.7 or more, the others of 0.3 or less.
All inputs are finite; a program needn't handle non-finite values.
Results may differ from the reference program's by a relative error of at most 0.00013.
Values sent between devices are 32-bit elements; how exact they have to be, the bound alone decides.
A program may use at most 32 MiB of HBM per device.

```python
import math
import jax
import jax.numpy as jnp
from jax import lax

NG = 12288
NP = 512
NW = 128
NB = 256
ITERS = 2
NV = 128
SLAB = 32
N_GRP = 48
N_COL = 8


def draw_band_energy(key, part):
    first, second = jax.random.split(jax.random.fold_in(key, 11))
    band_index = jnp.arange(NB)
    lower = jax.random.uniform(first, (NB,), jnp.float32, -2.0, -0.1)
    upper = jax.random.uniform(second, (NB,), jnp.float32, 0.2, 2.5)
    return jnp.where(band_index < NV, lower, upper)


def draw_band_occ(key, part):
    first, second = jax.random.split(jax.random.fold_in(key, 23))
    band_index = jnp.arange(NB)
    lower = jax.random.uniform(first, (NB,), jnp.float32, 0.7, 1.0)
    upper = jax.random.uniform(second, (NB,), jnp.float32, 0.0, 0.3)
    return jnp.where(band_index < NV, lower, upper)


def set_ends(drawn, rng, least, high):
    longest = drawn.shape.index(max(drawn.shape))
    spots = []
    for shift in (0, 1):
        where = [jax.random.randint(jax.random.fold_in(rng, axis), (), 0, length) for axis, length in enumerate(drawn.shape)]
        where[longest] = (where[longest] + shift) % drawn.shape[longest]
        spots.append(tuple(where))
    return drawn.at[spots[0]].set(least).at[spots[1]].set(high)


def block_scale(rng, dims, shards, least, high):
    loudness = 1.0
    for position, blocks in shards:
        heights = jax.random.uniform(jax.random.fold_in(jax.random.fold_in(rng, 6), position), (blocks,), jnp.float32, least / len(shards), high / len(shards))
        loudness = loudness * jnp.repeat(jnp.exp(heights), dims[position] // blocks).reshape((-1,) + (1,) * (len(dims) - 1 - position))
    return loudness


def noise(stream_key, extent, deviation, bound, shards=(), held_as=jnp.bfloat16):
    array = deviation * jax.random.normal(stream_key, extent, jnp.float32)
    if shards:
        array = array * block_scale(stream_key, extent, shards, -0.22, 0.18)
    return jnp.clip(array, -bound, bound).astype(held_as)


def setup_inputs(seed: int = 0) -> dict:
    streams_of = jax.random.split(jax.random.key(seed), 10)
    return {
        "rho_re": noise(streams_of[0], (NG, NP), (NG // 2) ** -0.5, 0.078125, ((0, 384), (1, 2)), jnp.float32),
        "rho_im": noise(streams_of[1], (NG, NP), (NG // 2) ** -0.5, 0.078125, ((0, 384), (1, 2)), jnp.float32),
        "coulomb": jnp.clip(jnp.exp(math.log(1.6) - 1.3862944 * jax.random.uniform(streams_of[2], (NG,), jnp.float32) ** block_scale(streams_of[2], (NG,), ((0, 768),), -0.2, 0.2)), 0.4, 1.6),
        "chi_prev": noise(streams_of[3], (2, N_GRP, N_COL, SLAB, NG), (16 * NG) ** -0.5, 0.013671875, ((2, 8), (3, 2), (4, 48)), jnp.float32),
        "source": noise(streams_of[4], (NG, NW), 1.0, 6.0, ((0, 768),), jnp.float32),
        "band_v": set_ends(jax.random.randint(streams_of[5], (NP,), 0, NV), jax.random.fold_in(streams_of[5], 1), 0, NV - 1).astype(jnp.int32),
        "band_c": set_ends(jax.random.randint(streams_of[6], (NP,), NV, NB), jax.random.fold_in(streams_of[6], 1), NV, NB - 1).astype(jnp.int32),
        "band_energy": draw_band_energy(jax.random.fold_in(streams_of[9], 71), 0),
        "band_occ": draw_band_occ(jax.random.fold_in(streams_of[9], 71), 0),
    }


frequency = 0.8
damping = 0.5


def pair_weight(band_v, band_c, band_energy, band_occ):
    delta = band_energy[band_c] - band_energy[band_v]
    filling = band_occ[band_v] - band_occ[band_c]
    return filling * 2.0 * delta / (delta * delta + frequency * frequency)


def contract(left, right):
    return lax.dot_general(left, right, (((0,), (0,)), ((), ())), precision=lax.Precision.HIGHEST, preferred_element_type=jnp.float32)


def matmul(left, right):
    return jnp.dot(left, right, precision=lax.Precision.HIGHEST, preferred_element_type=jnp.float32)


def reference(rho_re, rho_im, coulomb, chi_prev, source, band_v, band_c, band_energy, band_occ):
    weight = pair_weight(band_v, band_c, band_energy, band_occ)
    previous = chi_prev.reshape(2, NG, NG)
    scale = coulomb[:, None]
    real_part = source
    imag_part = jnp.zeros_like(source)
    for sweep in range(ITERS):
        scaled_re = scale * real_part
        scaled_im = scale * imag_part
        image_re = contract(previous[0], scaled_re) - contract(previous[1], scaled_im)
        image_im = contract(previous[0], scaled_im) + contract(previous[1], scaled_re)
        proj_re = contract(rho_re, scaled_re) + contract(rho_im, scaled_im)
        proj_im = contract(rho_re, scaled_im) - contract(rho_im, scaled_re)
        proj_re = weight[:, None] * proj_re
        proj_im = weight[:, None] * proj_im
        image_re = image_re - (matmul(rho_re, proj_re) - matmul(rho_im, proj_im))
        image_im = image_im - (matmul(rho_re, proj_im) + matmul(rho_im, proj_re))
        image_re = scale * image_re
        image_im = scale * image_im
        real_part = real_part + damping * (source + image_re - real_part)
        imag_part = imag_part + damping * (image_im - imag_part)
    return real_part, imag_part
```

```python
import functools

import jax
import jax.numpy as jnp
from jax import lax
from jax.experimental import pallas as pl
from jax.experimental.pallas import tpu as pltpu
from jax.sharding import PartitionSpec as P

ITERS = 2
NX = 4
NZ = 6
NC = 2
W = 128
frequency = 0.8
damping = 0.5
F32 = jnp.float32
BF16 = jnp.bfloat16
MESH = pl.DeviceIdType.MESH


def split(value):
    high = value.astype(BF16)
    low = (value - high.astype(F32)).astype(BF16)
    return high, low


def dot(left, right):
    return jnp.dot(left, right, preferred_element_type=F32)


def column(row):
    n = row.shape[1]
    down = lax.broadcasted_iota(jnp.int32, (n, n), 0)
    across = lax.broadcasted_iota(jnp.int32, (n, n), 1)
    return jnp.sum(jnp.where(down == across, row, 0.0), axis=1, keepdims=True)


def kernel(ny, rho_re, rho_im, coulomb, chi_prev, source, band_v, band_c, energy, occ,
           out_re, out_im,
           tile, wide_hi, wide_lo, pairs_t, pairs_w_hi, pairs_w_lo, both, grid1, grid2,
           part0, sib_in, part1, x_in, part2, y_in, z_all, full, sums, sums_in, halves, scaled, state, last, last_in,
           tile_sem, both_sem, gz_send, gx_send, gs_send, g_recv, gs_recv,
           sib_sem, xr_send, xr_recv, yr_send, yr_recv, za_send, za_recv, yg_send, yg_recv,
           xg_send, xg_recv, sg_send, sg_recv, rs_send, rs_recv, h_sem):
    grp = lax.axis_index("grp")
    my_y = lax.axis_index("col")
    my_k = lax.axis_index("dev")
    my_c = lax.rem(grp, NC)
    my_z = lax.rem(lax.div(grp, NC), NZ)
    my_x = lax.div(grp, NC * NZ)
    other_c = 1 - my_c
    other_k = 1 - my_k
    groups = NX * NZ * NC
    n_pairs = rho_re.shape[1]
    n_tiles = full.shape[3]
    per_y = n_tiles // ny
    block = tile.shape[4]

    def at(x=None, y=None, z=None, c=None, k=None):
        x = my_x if x is None else x
        y = my_y if y is None else y
        z = my_z if z is None else z
        c = my_c if c is None else c
        k = my_k if k is None else k
        return ((x * NZ + z) * NC + c, y, k)

    x_peers = [lax.rem(my_x + d, NX) for d in range(1, NX)]
    y_peers = [lax.rem(my_y + d, ny) for d in range(1, ny)]
    z_peers = [lax.rem(my_z + d, NZ) for d in range(1, NZ)]
    everyone = (
        [at(x=x) for x in x_peers]
        + [at(y=y) for y in y_peers]
        + [at(z=z) for z in z_peers]
        + [at(c=other_c), at(k=other_k)]
    )

    def remote(src, dst, send, recv, device):
        return pltpu.make_async_remote_copy(
            src_ref=src, dst_ref=dst, send_sem=send, recv_sem=recv, device_id=device, device_id_type=MESH
        )

    sent = []

    def send(src, dst, s, r, device):
        copy = remote(src, dst, s, r, device)
        copy.start()
        sent.append(copy)

    def arrive(dst, s, r):
        remote(dst, dst, s, r, at(c=other_c)).wait_recv()

    load = pltpu.make_async_copy(chi_prev, tile, tile_sem)
    load.start()

    scale16 = column(coulomb[...])
    src16 = source[...]
    both[my_k] = jnp.concatenate([src16, jnp.broadcast_to(scale16, (16, W))], axis=1)
    grid1[my_c, my_x, my_z] = scale16 * src16

    barrier = pltpu.get_barrier_semaphore()
    for device in everyone:
        pl.semaphore_signal(barrier, inc=1, device_id=device, device_id_type=MESH)
    pl.semaphore_wait(barrier, len(everyone))

    send(both.at[my_k], both.at[my_k], both_sem.at[0], both_sem.at[1], at(k=other_k))

    def gather_start(grid, i):
        own = grid.at[my_c, my_x, my_z]
        for j, z in enumerate(z_peers):
            send(own, own, gz_send.at[i, j], g_recv.at[i, my_x, my_z], at(z=z))
        for j, x in enumerate(x_peers):
            send(own, own, gx_send.at[i, j, my_z], g_recv.at[i, my_x, my_z], at(x=x))

    def gather_z(grid, i):
        def relay(z):
            held = grid.at[my_c, my_x, z]
            arrive(held, gz_send.at[i, 0], g_recv.at[i, my_x, z])
            for j, x in enumerate(x_peers):
                remote(held, held, gx_send.at[i, j, z], g_recv.at[i, my_x, z], at(x=x)).start()

        for d in range(1, NZ):
            @pl.when(my_z + d < NZ)
            def _():
                relay(my_z + d)

            @pl.when(my_z - d >= 0)
            def _():
                relay(my_z - d)

        row = grid.at[my_c, my_x]
        send(row, row, gs_send.at[i, my_x], gs_recv.at[i, my_x], at(c=other_c))

    def gather_x(grid, i):
        for j in (0, NX - 2, 1) if NX == 4 else range(NX - 1):
            x = x_peers[j]
            for z in range(NZ):
                arrive(grid.at[my_c, x, z], gz_send.at[i, 0], g_recv.at[i, x, z])
            row = grid.at[my_c, x]
            send(row, row, gs_send.at[i, x], gs_recv.at[i, x], at(c=other_c))

    def gather_end(grid, i):
        for x in range(NX):
            arrive(grid.at[other_c, x], gs_send.at[i, 0], gs_recv.at[i, x])
        value = jnp.concatenate(
            [grid[c, x, z] for x in range(NX) for z in range(NZ) for c in range(NC)], axis=0
        )
        return split(value)

    def gather_close(grid, i):
        for j, x in enumerate(x_peers):
            for d in range(1, NZ):
                z = z_peers[d - 1]
                held = grid.at[my_c, my_x, z]
                remote(held, held, gx_send.at[i, j, z], g_recv.at[i, my_x, z], at(x=x)).wait_send()

    def project(v_re, v_im, i):
        stacked = jnp.concatenate(
            [jnp.concatenate([v_re, v_im], axis=1), jnp.concatenate([v_im, -v_re], axis=1)], axis=0
        )
        high, low = split(stacked)
        value = dot(pairs_t[...], jnp.concatenate([high, high, low], axis=0))
        count = n_pairs // NC // NX
        for c in range(NC):
            for x in range(NX):
                for t in range(n_tiles):
                    row = (c * NX + x) * count + (t // 2) * 8
                    lane = (t % 2) * W
                    part0[i, c, x, t] = value[row : row + 8, lane : lane + W]
        send(part0.at[i, other_c], sib_in.at[i], sib_sem.at[0, i], sib_sem.at[1, i], at(c=other_c))

    def reduce_x(i):
        arrive(sib_in.at[i], sib_sem.at[0, i], sib_sem.at[1, i])
        part1[i] = part0[i, my_c] + sib_in[i]
        for j, x in enumerate(x_peers):
            send(part1.at[i, x], x_in.at[i, my_x], xr_send.at[i, j], xr_recv.at[i, my_x], at(x=x))

    def reduce_y(i):
        total = part1[i, my_x]
        for x in x_peers:
            arrive(x_in.at[i, x], xr_send.at[i, 0], xr_recv.at[i, x])
            total = total + x_in[i, x]
        part2[i] = total.reshape(part2.shape[1:])
        for j, y in enumerate(y_peers):
            send(part2.at[i, y], y_in.at[i, my_y], yr_send.at[i, j], yr_recv.at[i, my_y], at(y=y))

    def reduce_z(i):
        total = part2[i, my_y]
        for y in y_peers:
            arrive(y_in.at[i, y], yr_send.at[i, 0], yr_recv.at[i, y])
            total = total + y_in[i, y]
        z_all[i, my_z] = total
        for j, z in enumerate(z_peers):
            send(z_all.at[i, my_z], z_all.at[i, my_z], za_send.at[i, j], za_recv.at[i, my_z], at(z=z))

    def spread_y(i):
        for z in z_peers:
            arrive(z_all.at[i, z], za_send.at[i, 0], za_recv.at[i, z])
        total = z_all[i, 0]
        for z in range(1, NZ):
            total = total + z_all[i, z]
        mine = pl.ds(my_y * per_y, per_y)
        full[i, my_c, my_x, mine] = total
        own = full.at[i, my_c, my_x, mine]
        for j, y in enumerate(y_peers):
            send(own, own, yg_send.at[i, j], yg_recv.at[i, my_y], at(y=y))

    def spread_x(i):
        for y in y_peers:
            arrive(full.at[i, my_c, my_x, pl.ds(y * per_y, per_y)], yg_send.at[i, 0], yg_recv.at[i, y])
        own = full.at[i, my_c, my_x]
        for j, x in enumerate(x_peers):
            send(own, own, xg_send.at[i, j], xg_recv.at[i, my_x], at(x=x))
        send(own, own, sg_send.at[i, my_x], sg_recv.at[i, my_x], at(c=other_c))

    def spread_core(i):
        for x in x_peers:
            held = full.at[i, my_c, x]
            arrive(held, xg_send.at[i, 0], xg_recv.at[i, x])
            send(held, held, sg_send.at[i, x], sg_recv.at[i, x], at(c=other_c))

    def expand(i):
        for x in range(NX):
            arrive(full.at[i, other_c, x], sg_send.at[i, 0], sg_recv.at[i, x])
        lanes = []
        for lane in range(2):
            lanes.append(jnp.concatenate(
                [full[i, c, x, t] for c in range(NC) for x in range(NX) for t in range(lane, n_tiles, 2)], axis=0
            ))
        high, low = split(jnp.concatenate(lanes, axis=1))
        left = pairs_w_hi[...]
        value = dot(left, high) + dot(left, low) + dot(pairs_w_lo[...], high)
        return value[:32, :W] - value[32:, W:], value[:32, W:] + value[32:, :W]

    def scatter_start(re, im, i):
        for y in range(ny):
            sums[i, y] = jnp.concatenate([re[y * 32 : y * 32 + 32], im[y * 32 : y * 32 + 32]], axis=1)
        for j, y in enumerate(y_peers):
            send(sums.at[i, y], sums_in.at[i, my_y], rs_send.at[i, j], rs_recv.at[i, my_y], at(y=y))

    def scatter_end(i):
        total = sums[i, my_y]
        for y in y_peers:
            arrive(sums_in.at[i, y], rs_send.at[i, 0], rs_recv.at[i, y])
            total = total + sums_in[i, y]
        return total

    gather_start(grid1, 0)

    down = lax.broadcasted_iota(jnp.int32, (energy.shape[1], n_pairs), 0)
    in_v = down == band_v[...]
    in_c = down == band_c[...]
    e_col = column(energy[...])
    o_col = column(occ[...])

    def pick(match, table):
        return jnp.sum(jnp.where(match, table, 0.0), axis=0, keepdims=True)

    delta = pick(in_c, e_col) - pick(in_v, e_col)
    filling = pick(in_v, o_col) - pick(in_c, o_col)
    weight = filling * 2.0 * delta / (delta * delta + frequency * frequency)
    stacked_pairs = jnp.concatenate([rho_re[...], rho_im[...]], axis=0)
    high, low = split(stacked_pairs)
    high, low = high.astype(F32), low.astype(F32)
    pairs_t[...] = jnp.concatenate([high, low, high], axis=0).T.astype(BF16)
    high, low = split(stacked_pairs * weight)
    pairs_w_hi[...] = high
    pairs_w_lo[...] = low

    load.wait()
    for part in range(2):
        for step in range(groups // 8):
            turned = tile[part, step * 8 : step * 8 + 8, 0].reshape(128, block).T
            high, low = split(turned)
            rows = pl.ds(part * block, block)
            lanes = pl.ds(step * 128, 128)
            wide_hi[rows, lanes] = high
            wide_lo[rows, lanes] = low

    arrive(both.at[other_k], both_sem.at[0], both_sem.at[1])
    held = both[...].reshape(32, 2 * W)
    src = held[:, :W]
    scale = held[:, W:]
    real_part = src
    imag_part = jnp.zeros_like(src)

    for i in range(ITERS):
        grid = grid1 if i == 0 else grid2
        v_re = scale * real_part
        v_im = scale * imag_part
        if i > 0:
            scaled[...] = jnp.concatenate([v_re, v_im], axis=1).reshape(scaled.shape)
            grid[my_c, my_x, my_z] = scaled[my_k]
            gather_start(grid, i)
        project(v_re, v_im, i)
        gather_z(grid, i)
        reduce_x(i)
        reduce_y(i)
        gather_x(grid, i)
        reduce_z(i)
        high, low = gather_end(grid, i)
        if i == 0:
            value = dot(wide_hi[...], jnp.concatenate([high, low], axis=1))
            value = value[:, :W] + value[:, W:] + dot(wide_lo[...], high)
            scatter_start(value[:block], value[block:], i)
        else:
            value = dot(wide_hi[...], high) + dot(wide_hi[...], low) + dot(wide_lo[...], high)
            scatter_start(value[:block, :W] - value[block:, W:], value[:block, W:] + value[block:, :W], i)
        spread_y(i)
        spread_x(i)
        total = scatter_end(i)
        spread_core(i)
        q_re, q_im = expand(i)
        total = total - jnp.concatenate([q_re, q_im], axis=1)
        if i < ITERS - 1:
            halves[my_k] = total
            send(halves.at[my_k], halves.at[my_k], h_sem.at[0, i], h_sem.at[1, i], at(k=other_k))
            arrive(halves.at[other_k], h_sem.at[0, i], h_sem.at[1, i])
            image = halves[0] + halves[1]
            image_re = scale * image[:, :W]
            image_im = scale * image[:, W:]
            real_part = real_part + damping * (src + image_re - real_part)
            imag_part = imag_part + damping * (image_im - imag_part)
            state[...] = jnp.concatenate([real_part, imag_part], axis=1).reshape(state.shape)
        else:
            last[...] = total.reshape(last.shape)
            send(last.at[other_k], last_in, h_sem.at[0, i], h_sem.at[1, i], at(k=other_k))
            arrive(last_in, h_sem.at[0, i], h_sem.at[1, i])
            image = scale16 * (last[my_k] + last_in[...])
            mine = state[my_k]
            out_re[...] = mine[:, :W] + damping * (src16 + image[:, :W] - mine[:, :W])
            out_im[...] = mine[:, W:] + damping * (image[:, W:] - mine[:, W:])

    for copy in sent:
        copy.wait_send()
    gather_close(grid1, 0)
    gather_close(grid2, 1)


def shards(ny, rho_re, rho_im, coulomb, chi_prev, source, band_v, band_c, energy, occ):
    n_pairs = rho_re.shape[1]
    groups, rows, block = chi_prev.shape[1], chi_prev.shape[3], chi_prev.shape[4]
    n_tiles = 2 * (n_pairs // NC // NX // 8)
    per_y = n_tiles // ny
    n = ITERS
    dma = pltpu.SemaphoreType.DMA
    vmem = pltpu.VMEM
    out = jax.ShapeDtypeStruct((rows, W), F32)
    in_vmem = pl.BlockSpec(memory_space=pltpu.VMEM)
    scratch = [
        vmem(chi_prev.shape, F32),
        vmem((2 * block, 16 * groups), BF16),
        vmem((2 * block, 16 * groups), BF16),
        vmem((n_pairs, 192), BF16),
        vmem((64, n_pairs), BF16),
        vmem((64, n_pairs), BF16),
        vmem((2, 16, 2 * W), F32),
        vmem((NC, NX, NZ, 16, W), F32),
        vmem((NC, NX, NZ, 16, 2 * W), F32),
        vmem((n, NC, NX, n_tiles, 8, W), F32),
        vmem((n, NX, n_tiles, 8, W), F32),
        vmem((n, NX, n_tiles, 8, W), F32),
        vmem((n, NX, n_tiles, 8, W), F32),
        vmem((n, ny, per_y, 8, W), F32),
        vmem((n, ny, per_y, 8, W), F32),
        vmem((n, NZ, per_y, 8, W), F32),
        vmem((n, NC, NX, n_tiles, 8, W), F32),
        vmem((n, ny, 32, 2 * W), F32),
        vmem((n, ny, 32, 2 * W), F32),
        vmem((2, 32, 2 * W), F32),
        vmem((2, 16, 2 * W), F32),
        vmem((2, 16, 2 * W), F32),
        vmem((2, 16, 2 * W), F32),
        vmem((16, 2 * W), F32),
        dma(()), dma((2,)),
        dma((n, NZ - 1)), dma((n, NX - 1, NZ)), dma((n, NX)), dma((n, NX, NZ)), dma((n, NX)),
        dma((2, n)), dma((n, NX - 1)), dma((n, NX)), dma((n, ny - 1)), dma((n, ny)),
        dma((n, NZ - 1)), dma((n, NZ)), dma((n, ny - 1)), dma((n, ny)),
        dma((n, NX - 1)), dma((n, NX)), dma((n, NX)), dma((n, NX)),
        dma((n, ny - 1)), dma((n, ny)), dma((2, n)),
    ]
    return pl.pallas_call(
        functools.partial(kernel, ny),
        out_shape=(out, out),
        in_specs=[in_vmem] * 3 + [pl.BlockSpec(memory_space=pl.ANY)] + [in_vmem] * 5,
        out_specs=(in_vmem, in_vmem),
        scratch_shapes=scratch,
        compiler_params=pltpu.CompilerParams(
            collective_id=0, has_side_effects=True, vmem_limit_bytes=48 * 1024 * 1024
        ),
        name="dyson",
    )(
        rho_re, rho_im, coulomb.reshape(1, -1), chi_prev, source,
        band_v.reshape(1, -1), band_c.reshape(1, -1), energy.reshape(1, -1), occ.reshape(1, -1),
    )


def solution(mesh):
    placed = (
        P(("grp", "col"), "dev"),
        P(("grp", "col"), "dev"),
        P(("grp", "col", "dev")),
        P(None, None, "col", "dev", "grp"),
        P(("grp", "col", "dev"), None),
        P("dev"),
        P("dev"),
        P(),
        P(),
    )
    return jax.shard_map(
        functools.partial(shards, mesh.shape["col"]),
        mesh=mesh,
        in_specs=placed,
        out_specs=(P(("grp", "col", "dev"), None), P(("grp", "col", "dev"), None)),
        check_vma=False,
    )
```

```python
import functools

import jax
import jax.numpy as jnp
from jax import lax
from jax.experimental import pallas as pl
from jax.experimental.pallas import tpu as pltpu
from jax.sharding import PartitionSpec as P

ITERS = 2
NX = 4
NZ = 6
NC = 2
W = 128
frequency = 0.8
damping = 0.5
F32 = jnp.float32
BF16 = jnp.bfloat16
MESH = pl.DeviceIdType.MESH


def split(value):
    high = value.astype(BF16)
    low = (value - high.astype(F32)).astype(BF16)
    return high, low


def dot(left, right):
    return jnp.dot(left, right, preferred_element_type=F32)


def column(row):
    n = row.shape[1]
    down = lax.broadcasted_iota(jnp.int32, (n, n), 0)
    across = lax.broadcasted_iota(jnp.int32, (n, n), 1)
    return jnp.sum(jnp.where(down == across, row, 0.0), axis=1, keepdims=True)


def kernel(ny, rho_re_hbm, rho_im_hbm, coulomb_hbm, chi_prev, source_hbm, band_v_hbm, band_c_hbm, energy_hbm, occ_hbm,
           out,
           dens, coulomb, source, band_v, band_c, energy, occ, in_sem,
           tile, wide_hi, wide_lo, pairs_t, pairs_w_hi, pairs_w_lo, both, grid1, grid2,
           part0, sib_in, part1, x_in, part2, y_in, z_all, full, sums, sums_in, halves, scaled, state, last, last_in,
           both_sem, gz_send, gx_send, gs_send, g_recv, gs_recv,
           sib_sem, xr_send, xr_recv, yr_send, yr_recv, za_send, za_recv, yg_send, yg_recv,
           xg_send, xg_recv, sg_send, sg_recv, rs_send, rs_recv, h_sem):
    grp = lax.axis_index("grp")
    my_y = lax.axis_index("col")
    my_k = lax.axis_index("dev")
    my_c = lax.rem(grp, NC)
    my_z = lax.rem(lax.div(grp, NC), NZ)
    my_x = lax.div(grp, NC * NZ)
    other_c = 1 - my_c
    other_k = 1 - my_k
    groups = NX * NZ * NC
    n_pairs = dens.shape[1]
    n_tiles = full.shape[3]
    per_y = n_tiles // ny
    block = tile.shape[4]

    def at(x=None, y=None, z=None, c=None, k=None):
        x = my_x if x is None else x
        y = my_y if y is None else y
        z = my_z if z is None else z
        c = my_c if c is None else c
        k = my_k if k is None else k
        return ((x * NZ + z) * NC + c, y, k)

    x_peers = [lax.rem(my_x + d, NX) for d in range(1, NX)]
    y_peers = [lax.rem(my_y + d, ny) for d in range(1, ny)]
    z_peers = [lax.rem(my_z + d, NZ) for d in range(1, NZ)]
    everyone = (
        [at(x=x) for x in x_peers]
        + [at(y=y) for y in y_peers]
        + [at(z=z) for z in z_peers]
        + [at(c=other_c), at(k=other_k)]
    )

    def remote(src, dst, send, recv, device):
        return pltpu.make_async_remote_copy(
            src_ref=src, dst_ref=dst, send_sem=send, recv_sem=recv, device_id=device, device_id_type=MESH
        )

    sent = []

    def send(src, dst, s, r, device):
        copy = remote(src, dst, s, r, device)
        copy.start()
        sent.append(copy)

    def arrive(dst, s, r):
        remote(dst, dst, s, r, at(c=other_c)).wait_recv()

    loads = [
        pltpu.make_async_copy(src, dst, in_sem.at[j])
        for j, (src, dst) in enumerate([
            (coulomb_hbm, coulomb), (source_hbm, source),
            (band_v_hbm, band_v), (band_c_hbm, band_c), (energy_hbm, energy), (occ_hbm, occ),
            (rho_re_hbm, dens.at[pl.ds(0, 32)]), (rho_im_hbm, dens.at[pl.ds(32, 32)]),
            (chi_prev, tile),
        ])
    ]
    for load in loads:
        load.start()
    barrier = pltpu.get_barrier_semaphore()
    for device in everyone:
        pl.semaphore_signal(barrier, inc=1, device_id=device, device_id_type=MESH)
    for load in loads[:2]:
        load.wait()

    scale16 = column(coulomb[...])
    src16 = source[...]
    both[my_k] = jnp.concatenate([src16, jnp.broadcast_to(scale16, (16, W))], axis=1)
    grid1[my_c, my_x, my_z] = scale16 * src16

    pl.semaphore_wait(barrier, len(everyone))

    send(both.at[my_k], both.at[my_k], both_sem.at[0], both_sem.at[1], at(k=other_k))

    def gather_start(grid, i):
        own = grid.at[my_c, my_x, my_z]
        for j, z in enumerate(z_peers):
            send(own, own, gz_send.at[i, j], g_recv.at[i, my_x, my_z], at(z=z))
        for j, x in enumerate(x_peers):
            send(own, own, gx_send.at[i, j, my_z], g_recv.at[i, my_x, my_z], at(x=x))

    def gather_z(grid, i):
        def relay(z):
            held = grid.at[my_c, my_x, z]
            arrive(held, gz_send.at[i, 0], g_recv.at[i, my_x, z])
            for j, x in enumerate(x_peers):
                remote(held, held, gx_send.at[i, j, z], g_recv.at[i, my_x, z], at(x=x)).start()

        for d in range(1, NZ):
            @pl.when(my_z + d < NZ)
            def _():
                relay(my_z + d)

            @pl.when(my_z - d >= 0)
            def _():
                relay(my_z - d)

        row = grid.at[my_c, my_x]
        send(row, row, gs_send.at[i, my_x], gs_recv.at[i, my_x], at(c=other_c))

    def gather_x(grid, i):
        for j in (0, NX - 2, 1) if NX == 4 else range(NX - 1):
            x = x_peers[j]
            for z in range(NZ):
                arrive(grid.at[my_c, x, z], gz_send.at[i, 0], g_recv.at[i, x, z])
            row = grid.at[my_c, x]
            send(row, row, gs_send.at[i, x], gs_recv.at[i, x], at(c=other_c))

    def gather_end(grid, i):
        for x in range(NX):
            arrive(grid.at[other_c, x], gs_send.at[i, 0], gs_recv.at[i, x])
        value = jnp.concatenate(
            [grid[c, x, z] for x in range(NX) for z in range(NZ) for c in range(NC)], axis=0
        )
        return split(value)

    def gather_close(grid, i):
        for j, x in enumerate(x_peers):
            for d in range(1, NZ):
                z = z_peers[d - 1]
                held = grid.at[my_c, my_x, z]
                remote(held, held, gx_send.at[i, j, z], g_recv.at[i, my_x, z], at(x=x)).wait_send()

    def project(v_re, v_im, i):
        stacked = jnp.concatenate(
            [jnp.concatenate([v_re, v_im], axis=1), jnp.concatenate([v_im, -v_re], axis=1)], axis=0
        )
        high, low = split(stacked)
        value = dot(pairs_t[...], jnp.concatenate([high, high, low], axis=0))
        count = n_pairs // NC // NX
        for c in range(NC):
            for x in range(NX):
                for t in range(n_tiles):
                    row = (c * NX + x) * count + (t // 2) * 8
                    lane = (t % 2) * W
                    part0[i, c, x, t] = value[row : row + 8, lane : lane + W]
        send(part0.at[i, other_c], sib_in.at[i], sib_sem.at[0, i], sib_sem.at[1, i], at(c=other_c))

    def reduce_x(i):
        arrive(sib_in.at[i], sib_sem.at[0, i], sib_sem.at[1, i])
        part1[i] = part0[i, my_c] + sib_in[i]
        for j, x in enumerate(x_peers):
            send(part1.at[i, x], x_in.at[i, my_x], xr_send.at[i, j], xr_recv.at[i, my_x], at(x=x))

    def reduce_y(i):
        total = part1[i, my_x]
        for x in x_peers:
            arrive(x_in.at[i, x], xr_send.at[i, 0], xr_recv.at[i, x])
            total = total + x_in[i, x]
        part2[i] = total.reshape(part2.shape[1:])
        for j, y in enumerate(y_peers):
            send(part2.at[i, y], y_in.at[i, my_y], yr_send.at[i, j], yr_recv.at[i, my_y], at(y=y))

    def reduce_z(i):
        total = part2[i, my_y]
        for y in y_peers:
            arrive(y_in.at[i, y], yr_send.at[i, 0], yr_recv.at[i, y])
            total = total + y_in[i, y]
        z_all[i, my_z] = total
        for j, z in enumerate(z_peers):
            send(z_all.at[i, my_z], z_all.at[i, my_z], za_send.at[i, j], za_recv.at[i, my_z], at(z=z))

    def spread_y(i):
        for z in z_peers:
            arrive(z_all.at[i, z], za_send.at[i, 0], za_recv.at[i, z])
        total = z_all[i, 0]
        for z in range(1, NZ):
            total = total + z_all[i, z]
        mine = pl.ds(my_y * per_y, per_y)
        full[i, my_c, my_x, mine] = total
        own = full.at[i, my_c, my_x, mine]
        for j, y in enumerate(y_peers):
            send(own, own, yg_send.at[i, j], yg_recv.at[i, my_y], at(y=y))

    def spread_x(i):
        for y in y_peers:
            arrive(full.at[i, my_c, my_x, pl.ds(y * per_y, per_y)], yg_send.at[i, 0], yg_recv.at[i, y])
        own = full.at[i, my_c, my_x]
        for j, x in enumerate(x_peers):
            send(own, own, xg_send.at[i, j], xg_recv.at[i, my_x], at(x=x))
        send(own, own, sg_send.at[i, my_x], sg_recv.at[i, my_x], at(c=other_c))

    def spread_core(i):
        for x in x_peers:
            held = full.at[i, my_c, x]
            arrive(held, xg_send.at[i, 0], xg_recv.at[i, x])
            send(held, held, sg_send.at[i, x], sg_recv.at[i, x], at(c=other_c))

    def expand(i):
        for x in range(NX):
            arrive(full.at[i, other_c, x], sg_send.at[i, 0], sg_recv.at[i, x])
        lanes = []
        for lane in range(2):
            lanes.append(jnp.concatenate(
                [full[i, c, x, t] for c in range(NC) for x in range(NX) for t in range(lane, n_tiles, 2)], axis=0
            ))
        high, low = split(jnp.concatenate(lanes, axis=1))
        left = pairs_w_hi[...]
        value = dot(left, high) + dot(left, low) + dot(pairs_w_lo[...], high)
        return value[:32, :W] - value[32:, W:], value[:32, W:] + value[32:, :W]

    def scatter_store(re, im, i):
        for y in range(ny):
            sums[i, y] = jnp.concatenate([re[y * 32 : y * 32 + 32], im[y * 32 : y * 32 + 32]], axis=1)

    def scatter_start(i):
        for j, y in enumerate(y_peers):
            send(sums.at[i, y], sums_in.at[i, my_y], rs_send.at[i, j], rs_recv.at[i, my_y], at(y=y))

    def scatter_end(i):
        total = sums[i, my_y]
        for y in y_peers:
            arrive(sums_in.at[i, y], rs_send.at[i, 0], rs_recv.at[i, y])
            total = total + sums_in[i, y]
        return total

    gather_start(grid1, 0)

    for load in loads[2:8]:
        load.wait()
    down = lax.broadcasted_iota(jnp.int32, (energy.shape[1], n_pairs), 0)
    in_v = down == band_v[...]
    in_c = down == band_c[...]
    e_col = column(energy[...])
    o_col = column(occ[...])

    def pick(match, table):
        return jnp.sum(jnp.where(match, table, 0.0), axis=0, keepdims=True)

    delta = pick(in_c, e_col) - pick(in_v, e_col)
    filling = pick(in_v, o_col) - pick(in_c, o_col)
    weight = filling * 2.0 * delta / (delta * delta + frequency * frequency)
    stacked_pairs = dens[...]
    high, low = split(stacked_pairs)
    high, low = high.astype(F32), low.astype(F32)
    pairs_t[...] = jnp.concatenate([high, low, high], axis=0).T.astype(BF16)
    high, low = split(stacked_pairs * weight)
    pairs_w_hi[...] = high
    pairs_w_lo[...] = low

    loads[8].wait()
    for part in range(2):
        for step in range(groups // 8):
            turned = tile[part, step * 8 : step * 8 + 8, 0].reshape(128, block).T
            high, low = split(turned)
            rows = pl.ds(part * block, block)
            lanes = pl.ds(step * 128, 128)
            wide_hi[rows, lanes] = high
            wide_lo[rows, lanes] = low

    gather_z(grid1, 0)
    arrive(both.at[other_k], both_sem.at[0], both_sem.at[1])
    held = both[...].reshape(32, 2 * W)
    src = held[:, :W]
    scale = held[:, W:]
    real_part = src
    imag_part = jnp.zeros_like(src)

    for i in range(ITERS):
        grid = grid1 if i == 0 else grid2
        v_re = scale * real_part
        v_im = scale * imag_part
        if i == 0:
            project(v_re, v_im, i)
            gather_x(grid, i)
            reduce_x(i)
            high, low = gather_end(grid, i)
            value = dot(wide_hi[...], jnp.concatenate([high, low], axis=1))
            value = value[:, :W] + value[:, W:] + dot(wide_lo[...], high)
            scatter_store(value[:block], value[block:], i)
            reduce_y(i)
            scatter_start(i)
            reduce_z(i)
            spread_y(i)
        else:
            scaled[...] = jnp.concatenate([v_re, v_im], axis=1).reshape(scaled.shape)
            grid[my_c, my_x, my_z] = scaled[my_k]
            gather_start(grid, i)
            project(v_re, v_im, i)
            reduce_x(i)
            gather_z(grid, i)
            reduce_y(i)
            gather_x(grid, i)
            reduce_z(i)
            high, low = gather_end(grid, i)
            value = dot(wide_hi[...], high) + dot(wide_hi[...], low) + dot(wide_lo[...], high)
            scatter_store(value[:block, :W] - value[block:, W:], value[:block, W:] + value[block:, :W], i)
            spread_y(i)
            scatter_start(i)
        spread_x(i)
        total = scatter_end(i)
        spread_core(i)
        q_re, q_im = expand(i)
        total = total - jnp.concatenate([q_re, q_im], axis=1)
        if i < ITERS - 1:
            halves[my_k] = total
            send(halves.at[my_k], halves.at[my_k], h_sem.at[0, i], h_sem.at[1, i], at(k=other_k))
            arrive(halves.at[other_k], h_sem.at[0, i], h_sem.at[1, i])
            image = halves[0] + halves[1]
            image_re = scale * image[:, :W]
            image_im = scale * image[:, W:]
            real_part = real_part + damping * (src + image_re - real_part)
            imag_part = imag_part + damping * (image_im - imag_part)
            state[...] = jnp.concatenate([real_part, imag_part], axis=1).reshape(state.shape)
        else:
            last[...] = total.reshape(last.shape)
            send(last.at[other_k], last_in, h_sem.at[0, i], h_sem.at[1, i], at(k=other_k))
            for copy in sent:
                copy.wait_send()
            gather_close(grid1, 0)
            gather_close(grid2, 1)
            arrive(last_in, h_sem.at[0, i], h_sem.at[1, i])
            image = scale16 * (last[my_k] + last_in[...])
            mine = state[my_k]
            out[0] = mine[:, :W] + damping * (src16 + image[:, :W] - mine[:, :W])
            out[1] = mine[:, W:] + damping * (image[:, W:] - mine[:, W:])


def shards(ny, rho_re, rho_im, coulomb, chi_prev, source, band_v, band_c, energy, occ):
    n_pairs = rho_re.shape[1]
    groups, rows, block = chi_prev.shape[1], chi_prev.shape[3], chi_prev.shape[4]
    n_tiles = 2 * (n_pairs // NC // NX // 8)
    per_y = n_tiles // ny
    n = ITERS
    dma = pltpu.SemaphoreType.DMA
    vmem = pltpu.VMEM
    out = jax.ShapeDtypeStruct((2, rows, W), F32)
    in_vmem = pl.BlockSpec(memory_space=pltpu.VMEM)
    scratch = [
        vmem((64, n_pairs), F32), vmem((1, 16), F32), vmem((rows, W), F32),
        vmem((1, n_pairs), jnp.int32), vmem((1, n_pairs), jnp.int32),
        vmem((1, energy.shape[0]), F32), vmem((1, energy.shape[0]), F32), dma((9,)),
        vmem(chi_prev.shape, F32),
        vmem((2 * block, 16 * groups), BF16),
        vmem((2 * block, 16 * groups), BF16),
        vmem((n_pairs, 192), BF16),
        vmem((64, n_pairs), BF16),
        vmem((64, n_pairs), BF16),
        vmem((2, 16, 2 * W), F32),
        vmem((NC, NX, NZ, 16, W), F32),
        vmem((NC, NX, NZ, 16, 2 * W), F32),
        vmem((n, NC, NX, n_tiles, 8, W), F32),
        vmem((n, NX, n_tiles, 8, W), F32),
        vmem((n, NX, n_tiles, 8, W), F32),
        vmem((n, NX, n_tiles, 8, W), F32),
        vmem((n, ny, per_y, 8, W), F32),
        vmem((n, ny, per_y, 8, W), F32),
        vmem((n, NZ, per_y, 8, W), F32),
        vmem((n, NC, NX, n_tiles, 8, W), F32),
        vmem((n, ny, 32, 2 * W), F32),
        vmem((n, ny, 32, 2 * W), F32),
        vmem((2, 32, 2 * W), F32),
        vmem((2, 16, 2 * W), F32),
        vmem((2, 16, 2 * W), F32),
        vmem((2, 16, 2 * W), F32),
        vmem((16, 2 * W), F32),
        dma((2,)),
        dma((n, NZ - 1)), dma((n, NX - 1, NZ)), dma((n, NX)), dma((n, NX, NZ)), dma((n, NX)),
        dma((2, n)), dma((n, NX - 1)), dma((n, NX)), dma((n, ny - 1)), dma((n, ny)),
        dma((n, NZ - 1)), dma((n, NZ)), dma((n, ny - 1)), dma((n, ny)),
        dma((n, NX - 1)), dma((n, NX)), dma((n, NX)), dma((n, NX)),
        dma((n, ny - 1)), dma((n, ny)), dma((2, n)),
    ]
    result = pl.pallas_call(
        functools.partial(kernel, ny),
        out_shape=out,
        in_specs=[pl.BlockSpec(memory_space=pltpu.HBM)] * 9,
        out_specs=in_vmem,
        scratch_shapes=scratch,
        compiler_params=pltpu.CompilerParams(
            collective_id=0, has_side_effects=True, vmem_limit_bytes=48 * 1024 * 1024
        ),
        name="dyson",
    )(
        *[
            pltpu.with_memory_space_constraint(operand, pltpu.HBM)
            for operand in (
                rho_re, rho_im, coulomb.reshape(1, -1), chi_prev, source,
                band_v.reshape(1, -1), band_c.reshape(1, -1), energy.reshape(1, -1), occ.reshape(1, -1),
            )
        ]
    )
    return result[0], result[1]


def solution(mesh):
    placed = (
        P(("grp", "col"), "dev"),
        P(("grp", "col"), "dev"),
        P(("grp", "col", "dev")),
        P(None, None, "col", "dev", "grp"),
        P(("grp", "col", "dev"), None),
        P("dev"),
        P("dev"),
        P(),
        P(),
    )
    return jax.shard_map(
        functools.partial(shards, mesh.shape["col"]),
        mesh=mesh,
        in_specs=placed,
        out_specs=(P(("grp", "col", "dev"), None), P(("grp", "col", "dev"), None)),
        check_vma=False,
    )
```

```python
import functools

import jax
import jax.numpy as jnp
from jax import lax
from jax.experimental import pallas as pl
from jax.experimental.pallas import tpu as pltpu
from jax.sharding import PartitionSpec as P

ITERS = 2
NX = 4
NZ = 6
NC = 2
W = 128
frequency = 0.8
damping = 0.5
F32 = jnp.float32
BF16 = jnp.bfloat16
MESH = pl.DeviceIdType.MESH


def split(value):
    high = value.astype(BF16)
    low = (value - high.astype(F32)).astype(BF16)
    return high, low


def dot(left, right):
    return jnp.dot(left, right, preferred_element_type=F32)


def column(row):
    n = row.shape[1]
    down = lax.broadcasted_iota(jnp.int32, (n, n), 0)
    across = lax.broadcasted_iota(jnp.int32, (n, n), 1)
    return jnp.sum(jnp.where(down == across, row, 0.0), axis=1, keepdims=True)


def kernel(ny, rho_re_hbm, rho_im_hbm, coulomb_hbm, chi_prev, source_hbm, band_v_hbm, band_c_hbm, energy_hbm, occ_hbm,
           out,
           dens, coulomb, source, band_v, band_c, energy, occ, in_sem,
           tile, wide_hi, wide_lo, pairs_t, pairs_w, both, grid1, grid2,
           part0, sib_in, part1, x_in, part2, y_in, z_all, full, sums, sums_in, halves, scaled, state, last, last_in, product,
           both_sem, w_sem, gz_send, gx_send, gs_send, g_recv, gs_recv,
           sib_send, sib_recv, xr_send, xr_recv, yr_send, yr_recv, za_send, za_recv, yg_send, yg_recv,
           xg_send, xg_recv, sg_send, sg_recv, rs_send, rs_recv, h_sem):
    grp = lax.axis_index("grp")
    my_y = lax.axis_index("col")
    my_k = lax.axis_index("dev")
    my_c = lax.rem(grp, NC)
    my_z = lax.rem(lax.div(grp, NC), NZ)
    my_x = lax.div(grp, NC * NZ)
    other_c = 1 - my_c
    other_k = 1 - my_k
    groups = NX * NZ * NC
    n_pairs = dens.shape[1]
    n_tiles = full.shape[3]
    per_y = n_tiles // ny
    block = tile.shape[4]

    def at(x=None, y=None, z=None, c=None, k=None):
        x = my_x if x is None else x
        y = my_y if y is None else y
        z = my_z if z is None else z
        c = my_c if c is None else c
        k = my_k if k is None else k
        return ((x * NZ + z) * NC + c, y, k)

    x_peers = [lax.rem(my_x + d, NX) for d in range(1, NX)]
    y_peers = [lax.rem(my_y + d, ny) for d in range(1, ny)]
    x_order = x_peers[1:2] + x_peers[:1] + x_peers[2:] + [my_x]
    z_peers = [lax.rem(my_z + d, NZ) for d in range(1, NZ)]
    ring = [(my_z, other_k)] + [(z, k) for z in z_peers for k in (other_k, my_k)]
    everyone = (
        [at(x=x) for x in x_peers]
        + [at(y=y) for y in y_peers]
        + [at(z=z) for z in z_peers]
        + [at(z=z, k=other_k) for z in z_peers]
        + [at(c=other_c), at(k=other_k)]
    )

    def remote(src, dst, send, recv, device):
        return pltpu.make_async_remote_copy(
            src_ref=src, dst_ref=dst, send_sem=send, recv_sem=recv, device_id=device, device_id_type=MESH
        )

    sent = []

    def send(src, dst, s, r, device):
        copy = remote(src, dst, s, r, device)
        copy.start()
        sent.append(copy)

    def arrive(dst, s, r):
        remote(dst, dst, s, r, at(c=other_c)).wait_recv()

    loads = [
        pltpu.make_async_copy(src, dst, in_sem.at[j])
        for j, (src, dst) in enumerate([
            (coulomb_hbm, coulomb), (source_hbm, source),
            (band_v_hbm, band_v), (band_c_hbm, band_c), (energy_hbm, energy), (occ_hbm, occ),
            (rho_re_hbm, dens.at[pl.ds(0, 32)]), (rho_im_hbm, dens.at[pl.ds(32, 32)]),
            (chi_prev, tile),
        ])
    ]
    for load in loads:
        load.start()
    barrier = pltpu.get_barrier_semaphore()
    for device in everyone:
        pl.semaphore_signal(barrier, inc=1, device_id=device, device_id_type=MESH)
    for load in loads[:2]:
        load.wait()

    scale16 = column(coulomb[...])
    src16 = source[...]
    both[my_k] = jnp.concatenate([src16, jnp.broadcast_to(scale16, (16, W))], axis=1)
    grid1[my_c, my_x, my_z] = scale16 * src16

    pl.semaphore_wait(barrier, len(everyone))

    send(both.at[my_k], both.at[my_k], both_sem.at[0], both_sem.at[1], at(k=other_k))

    def gather_start(grid, i):
        own = grid.at[my_c, my_x, my_z]
        for j, z in enumerate(z_peers):
            send(own, own, gz_send.at[i, j], g_recv.at[i, my_x, my_z], at(z=z))
        for j, x in enumerate(x_peers):
            send(own, own, gx_send.at[i, j, my_z], g_recv.at[i, my_x, my_z], at(x=x))

    def gather_z(grid, i):
        def relay(z):
            held = grid.at[my_c, my_x, z]
            arrive(held, gz_send.at[i, 0], g_recv.at[i, my_x, z])
            for j, x in enumerate(x_peers):
                remote(held, held, gx_send.at[i, j, z], g_recv.at[i, my_x, z], at(x=x)).start()

        for d in range(1, NZ):
            @pl.when(my_z + d < NZ)
            def _():
                relay(my_z + d)

            @pl.when(my_z - d >= 0)
            def _():
                relay(my_z - d)

        row = grid.at[my_c, my_x]
        send(row, row, gs_send.at[i, my_x], gs_recv.at[i, my_x], at(c=other_c))

    def gather_x(grid, i):
        for j in (0, NX - 2, 1) if NX == 4 else range(NX - 1):
            x = x_peers[j]
            for z in range(NZ):
                arrive(grid.at[my_c, x, z], gz_send.at[i, 0], g_recv.at[i, x, z])
            row = grid.at[my_c, x]
            send(row, row, gs_send.at[i, x], gs_recv.at[i, x], at(c=other_c))

    def gather_end(grid, i):
        for x in range(NX):
            arrive(grid.at[other_c, x], gs_send.at[i, 0], gs_recv.at[i, x])
        value = jnp.concatenate(
            [grid[c, x, z] for x in range(NX) for z in range(NZ) for c in range(NC)], axis=0
        )
        return split(value)

    def gather_close(grid, i):
        for j, x in enumerate(x_peers):
            for d in range(1, NZ):
                z = z_peers[d - 1]
                held = grid.at[my_c, my_x, z]
                remote(held, held, gx_send.at[i, j, z], g_recv.at[i, my_x, z], at(x=x)).wait_send()

    def project(v_re, v_im, i):
        stacked = jnp.concatenate(
            [jnp.concatenate([v_re, v_im], axis=1), jnp.concatenate([v_im, -v_re], axis=1)], axis=0
        )
        high, low = split(stacked)
        value = dot(pairs_t[...], jnp.concatenate([high, high, low], axis=0))
        count = n_pairs // NC // NX
        for c in range(NC):
            for x in range(NX):
                for t in range(n_tiles):
                    row = (c * NX + x) * count + (t // 2) * 8
                    lane = (t % 2) * W
                    part0[i, c, x, t] = value[row : row + 8, lane : lane + W]
        for x in x_order:
            send(part0.at[i, other_c, x], sib_in.at[i, x], sib_send.at[i, x], sib_recv.at[i, x], at(c=other_c))

    def reduce_x(i):
        for j, x in enumerate(x_order):
            arrive(sib_in.at[i, x], sib_send.at[i, x], sib_recv.at[i, x])
            part1[i, x] = part0[i, my_c, x] + sib_in[i, x]
            if j == NX - 1:
                continue
            send(part1.at[i, x], x_in.at[i, my_x], xr_send.at[i, j], xr_recv.at[i, my_x], at(x=x))

    def reduce_y(i):
        total = part1[i, my_x]
        for x in x_peers:
            arrive(x_in.at[i, x], xr_send.at[i, 0], xr_recv.at[i, x])
            total = total + x_in[i, x]
        part2[i] = total.reshape(part2.shape[1:])
        for j, y in enumerate(y_peers):
            send(part2.at[i, y], y_in.at[i, my_y], yr_send.at[i, j], yr_recv.at[i, my_y], at(y=y))

    def reduce_z(i):
        total = part2[i, my_y]
        for y in y_peers:
            arrive(y_in.at[i, y], yr_send.at[i, 0], yr_recv.at[i, y])
            total = total + y_in[i, y]
        z_all[i, my_k, my_z] = total
        own = z_all.at[i, my_k, my_z]
        for j, (z, k) in enumerate(ring):
            send(own, own, za_send.at[i, j], za_recv.at[i, my_k, my_z], at(z=z, k=k))

    def spread_y(i):
        for z, k in ring:
            arrive(z_all.at[i, k, z], za_send.at[i, 0], za_recv.at[i, k, z])
        for k in range(2):
            total = z_all[i, k, 0]
            for z in range(1, NZ):
                total = total + z_all[i, k, z]
            for t in range(per_y):
                full[i, my_c, my_x, my_y * per_y + t, k] = total[t]
        own = full.at[i, my_c, my_x, pl.ds(my_y * per_y, per_y)]
        for j, y in enumerate(y_peers):
            send(own, own, yg_send.at[i, j], yg_recv.at[i, my_y], at(y=y))

    def spread_x(i):
        for y in y_peers:
            arrive(full.at[i, my_c, my_x, pl.ds(y * per_y, per_y)], yg_send.at[i, 0], yg_recv.at[i, y])
        own = full.at[i, my_c, my_x]
        for j, x in enumerate(x_peers):
            send(own, own, xg_send.at[i, j], xg_recv.at[i, my_x], at(x=x))
        send(own, own, sg_send.at[i, my_x], sg_recv.at[i, my_x], at(c=other_c))

    def spread_core(i):
        for x in x_peers:
            held = full.at[i, my_c, x]
            arrive(held, xg_send.at[i, 0], xg_recv.at[i, x])
            send(held, held, sg_send.at[i, x], sg_recv.at[i, x], at(c=other_c))

    def expand(i):
        for x in range(NX):
            arrive(full.at[i, other_c, x], sg_send.at[i, 0], sg_recv.at[i, x])
        lanes = []
        for lane in range(2):
            lanes.append(jnp.concatenate(
                [full[i, c, x, t, k]
                 for k in range(2) for c in range(NC) for x in range(NX) for t in range(lane, n_tiles, 2)], axis=0
            ))
        high, low = split(jnp.concatenate(lanes, axis=1))
        left_hi, left_lo = split(jnp.concatenate([pairs_w[0], pairs_w[1]], axis=1))
        value = dot(left_hi, high) + dot(left_hi, low) + dot(left_lo, high)
        return jnp.concatenate(
            [value[:32, :W] - value[32:, W:], value[:32, W:] + value[32:, :W]], axis=1
        )

    def scatter_store(re, im, i):
        for y in range(ny):
            sums[i, y] = jnp.concatenate([re[y * 32 : y * 32 + 32], im[y * 32 : y * 32 + 32]], axis=1)

    def scatter_start(i):
        for j, y in enumerate(y_peers):
            send(sums.at[i, y], sums_in.at[i, my_y], rs_send.at[i, j], rs_recv.at[i, my_y], at(y=y))

    def scatter_end(i):
        total = sums[i, my_y]
        for y in y_peers:
            arrive(sums_in.at[i, y], rs_send.at[i, 0], rs_recv.at[i, y])
            total = total + sums_in[i, y]
        return total

    gather_start(grid1, 0)

    for load in loads[2:8]:
        load.wait()
    down = lax.broadcasted_iota(jnp.int32, (energy.shape[1], n_pairs), 0)
    in_v = down == band_v[...]
    in_c = down == band_c[...]
    e_col = column(energy[...])
    o_col = column(occ[...])

    def pick(match, table):
        return jnp.sum(jnp.where(match, table, 0.0), axis=0, keepdims=True)

    delta = pick(in_c, e_col) - pick(in_v, e_col)
    filling = pick(in_v, o_col) - pick(in_c, o_col)
    weight = filling * 2.0 * delta / (delta * delta + frequency * frequency)
    stacked_pairs = dens[...]
    high, low = split(stacked_pairs)
    high, low = high.astype(F32), low.astype(F32)
    pairs_t[...] = jnp.concatenate([high, low, high], axis=0).T.astype(BF16)
    pairs_w[my_k] = stacked_pairs * weight

    loads[8].wait()
    for part in range(2):
        for step in range(groups // 8):
            turned = tile[part, step * 8 : step * 8 + 8, 0].reshape(128, block).T
            high, low = split(turned)
            rows = pl.ds(part * block, block)
            lanes = pl.ds(step * 128, 128)
            wide_hi[rows, lanes] = high
            wide_lo[rows, lanes] = low

    gather_z(grid1, 0)
    arrive(both.at[other_k], both_sem.at[0], both_sem.at[1])
    held = both[...].reshape(32, 2 * W)
    src = held[:, :W]
    scale = held[:, W:]
    real_part = src
    imag_part = jnp.zeros_like(src)

    for i in range(ITERS):
        grid = grid1 if i == 0 else grid2
        v_re = scale * real_part
        v_im = scale * imag_part
        if i == 0:
            project(v_re, v_im, i)
            gather_x(grid, i)
            reduce_x(i)
            send(pairs_w.at[my_k], pairs_w.at[my_k], w_sem.at[0], w_sem.at[1], at(k=other_k))
            high, low = gather_end(grid, i)
            value = dot(wide_hi[...], jnp.concatenate([high, low], axis=1))
            value = value[:, :W] + value[:, W:] + dot(wide_lo[...], high)
            scatter_store(value[:block], value[block:], i)
            reduce_y(i)
            scatter_start(i)
            reduce_z(i)
        else:
            scaled[...] = jnp.concatenate([v_re, v_im], axis=1).reshape(scaled.shape)
            grid[my_c, my_x, my_z] = scaled[my_k]
            gather_start(grid, i)
            project(v_re, v_im, i)
            reduce_x(i)
            gather_z(grid, i)
            reduce_y(i)
            gather_x(grid, i)
            reduce_z(i)
            high, low = gather_end(grid, i)
            value = dot(wide_hi[...], high) + dot(wide_hi[...], low) + dot(wide_lo[...], high)
            scatter_store(value[:block, :W] - value[block:, W:], value[:block, W:] + value[block:, :W], i)
            scatter_start(i)
        spread_y(i)
        if i < ITERS - 1:
            halves[my_k] = scatter_end(i)
            send(halves.at[my_k], halves.at[my_k], h_sem.at[0, i], h_sem.at[1, i], at(k=other_k))
            spread_x(i)
            spread_core(i)
            arrive(halves.at[other_k], h_sem.at[0, i], h_sem.at[1, i])
            arrive(pairs_w.at[other_k], w_sem.at[0], w_sem.at[1])
            image = halves[0] + halves[1] - expand(i)
            real_part = real_part + damping * (src + scale * image[:, :W] - real_part)
            imag_part = imag_part + damping * (scale * image[:, W:] - imag_part)
            state[...] = jnp.concatenate([real_part, imag_part], axis=1).reshape(state.shape)
        else:
            last[...] = scatter_end(i).reshape(last.shape)
            send(last.at[other_k], last_in, h_sem.at[0, i], h_sem.at[1, i], at(k=other_k))
            spread_x(i)
            spread_core(i)
            for copy in sent:
                copy.wait_send()
            gather_close(grid1, 0)
            gather_close(grid2, 1)
            arrive(last_in, h_sem.at[0, i], h_sem.at[1, i])
            product[...] = expand(i).reshape(product.shape)
            image = scale16 * (last[my_k] + last_in[...] - product[my_k])
            mine = state[my_k]
            out[0] = mine[:, :W] + damping * (src16 + image[:, :W] - mine[:, :W])
            out[1] = mine[:, W:] + damping * (image[:, W:] - mine[:, W:])


def shards(ny, rho_re, rho_im, coulomb, chi_prev, source, band_v, band_c, energy, occ):
    n_pairs = rho_re.shape[1]
    groups, rows, block = chi_prev.shape[1], chi_prev.shape[3], chi_prev.shape[4]
    n_tiles = 2 * (n_pairs // NC // NX // 8)
    per_y = n_tiles // ny
    n = ITERS
    dma = pltpu.SemaphoreType.DMA
    vmem = pltpu.VMEM
    out = jax.ShapeDtypeStruct((2, rows, W), F32)
    in_vmem = pl.BlockSpec(memory_space=pltpu.VMEM)
    scratch = [
        vmem((64, n_pairs), F32), vmem((1, 16), F32), vmem((rows, W), F32),
        vmem((1, n_pairs), jnp.int32), vmem((1, n_pairs), jnp.int32),
        vmem((1, energy.shape[0]), F32), vmem((1, energy.shape[0]), F32), dma((9,)),
        vmem(chi_prev.shape, F32),
        vmem((2 * block, 16 * groups), BF16),
        vmem((2 * block, 16 * groups), BF16),
        vmem((n_pairs, 192), BF16),
        vmem((2, 64, n_pairs), F32),
        vmem((2, 16, 2 * W), F32),
        vmem((NC, NX, NZ, 16, W), F32),
        vmem((NC, NX, NZ, 16, 2 * W), F32),
        vmem((n, NC, NX, n_tiles, 8, W), F32),
        vmem((n, NX, n_tiles, 8, W), F32),
        vmem((n, NX, n_tiles, 8, W), F32),
        vmem((n, NX, n_tiles, 8, W), F32),
        vmem((n, ny, per_y, 8, W), F32),
        vmem((n, ny, per_y, 8, W), F32),
        vmem((n, 2, NZ, per_y, 8, W), F32),
        vmem((n, NC, NX, n_tiles, 2, 8, W), F32),
        vmem((n, ny, 32, 2 * W), F32),
        vmem((n, ny, 32, 2 * W), F32),
        vmem((2, 32, 2 * W), F32),
        vmem((2, 16, 2 * W), F32),
        vmem((2, 16, 2 * W), F32),
        vmem((2, 16, 2 * W), F32),
        vmem((16, 2 * W), F32),
        vmem((2, 16, 2 * W), F32),
        dma((2,)), dma((2,)),
        dma((n, NZ - 1)), dma((n, NX - 1, NZ)), dma((n, NX)), dma((n, NX, NZ)), dma((n, NX)),
        dma((n, NX)), dma((n, NX)), dma((n, NX - 1)), dma((n, NX)), dma((n, ny - 1)), dma((n, ny)),
        dma((n, 2 * NZ - 1)), dma((n, 2, NZ)), dma((n, ny - 1)), dma((n, ny)),
        dma((n, NX - 1)), dma((n, NX)), dma((n, NX)), dma((n, NX)),
        dma((n, ny - 1)), dma((n, ny)), dma((2, n)),
    ]
    result = pl.pallas_call(
        functools.partial(kernel, ny),
        out_shape=out,
        in_specs=[pl.BlockSpec(memory_space=pltpu.HBM)] * 9,
        out_specs=in_vmem,
        scratch_shapes=scratch,
        compiler_params=pltpu.CompilerParams(
            collective_id=0, has_side_effects=True, vmem_limit_bytes=48 * 1024 * 1024
        ),
        name="dyson",
    )(
        *[
            pltpu.with_memory_space_constraint(operand, pltpu.HBM)
            for operand in (
                rho_re, rho_im, coulomb.reshape(1, -1), chi_prev, source,
                band_v.reshape(1, -1), band_c.reshape(1, -1), energy.reshape(1, -1), occ.reshape(1, -1),
            )
        ]
    )
    return result[0], result[1]


def solution(mesh):
    placed = (
        P(("grp", "col"), "dev"),
        P(("grp", "col"), "dev"),
        P(("grp", "col", "dev")),
        P(None, None, "col", "dev", "grp"),
        P(("grp", "col", "dev"), None),
        P("dev"),
        P("dev"),
        P(),
        P(),
    )
    return jax.shard_map(
        functools.partial(shards, mesh.shape["col"]),
        mesh=mesh,
        in_specs=placed,
        out_specs=(P(("grp", "col", "dev"), None), P(("grp", "col", "dev"), None)),
        check_vma=False,
    )
```

```python
import functools

import jax
import jax.numpy as jnp
from jax import lax
from jax.experimental import pallas as pl
from jax.experimental.pallas import tpu as pltpu
from jax.sharding import PartitionSpec as P

ITERS = 2
NX = 4
NZ = 6
NC = 2
W = 128
frequency = 0.8
damping = 0.5
F32 = jnp.float32
BF16 = jnp.bfloat16
MESH = pl.DeviceIdType.MESH


def split(value):
    high = value.astype(BF16)
    low = (value - high.astype(F32)).astype(BF16)
    return high, low


def dot(left, right):
    return jnp.dot(left, right, preferred_element_type=F32)


def column(row):
    n = row.shape[1]
    down = lax.broadcasted_iota(jnp.int32, (n, n), 0)
    across = lax.broadcasted_iota(jnp.int32, (n, n), 1)
    return jnp.sum(jnp.where(down == across, row, 0.0), axis=1, keepdims=True)


def kernel(ny, rho_re_hbm, rho_im_hbm, coulomb_hbm, chi_prev, source_hbm, band_v_hbm, band_c_hbm, energy_hbm, occ_hbm,
           out,
           dens, coulomb, source, band_v, band_c, energy, occ, in_sem,
           tile, wide_hi, wide_lo, pairs_t, pairs_w, both, grid1, grid2,
           part0, sib_in, part1, x_in, part2, y_in, z_all, full, sums, sums_in, halves, scaled, state, last, last_in, product,
           both_sem, w_sem, gz_send, gx_send, gs_send, g_recv, gs_recv,
           sib_send, sib_recv, xr_send, xr_recv, yr_send, yr_recv, za_send, za_recv, yg_send, yg_recv,
           xg_send, xg_recv, sg_send, sg_recv, rs_send, rs_recv, h_sem):
    grp = lax.axis_index("grp")
    my_y = lax.axis_index("col")
    my_k = lax.axis_index("dev")
    my_c = lax.rem(grp, NC)
    my_z = lax.rem(lax.div(grp, NC), NZ)
    my_x = lax.div(grp, NC * NZ)
    other_c = 1 - my_c
    other_k = 1 - my_k
    groups = NX * NZ * NC
    n_pairs = dens.shape[1]
    n_tiles = full.shape[3]
    per_y = n_tiles // ny
    block = tile.shape[4]

    def at(x=None, y=None, z=None, c=None, k=None):
        x = my_x if x is None else x
        y = my_y if y is None else y
        z = my_z if z is None else z
        c = my_c if c is None else c
        k = my_k if k is None else k
        return ((x * NZ + z) * NC + c, y, k)

    x_peers = [lax.rem(my_x + d, NX) for d in range(1, NX)]
    y_peers = [lax.rem(my_y + d, ny) for d in range(1, ny)]
    x_order = x_peers[1:2] + x_peers[:1] + x_peers[2:] + [my_x]
    z_peers = [lax.rem(my_z + d, NZ) for d in range(1, NZ)]
    ring = [(my_z, other_k)] + [(z, k) for z in z_peers for k in (other_k, my_k)]
    everyone = (
        [at(x=x) for x in x_peers]
        + [at(y=y) for y in y_peers]
        + [at(z=z) for z in z_peers]
        + [at(z=z, k=other_k) for z in z_peers]
        + [at(c=other_c), at(k=other_k)]
    )

    def remote(src, dst, send, recv, device):
        return pltpu.make_async_remote_copy(
            src_ref=src, dst_ref=dst, send_sem=send, recv_sem=recv, device_id=device, device_id_type=MESH
        )

    sent = []

    def send(src, dst, s, r, device):
        copy = remote(src, dst, s, r, device)
        copy.start()
        sent.append(copy)

    def arrive(dst, s, r):
        remote(dst, dst, s, r, at(c=other_c)).wait_recv()

    loads = [
        pltpu.make_async_copy(src, dst, in_sem.at[j])
        for j, (src, dst) in enumerate([
            (coulomb_hbm, coulomb), (source_hbm, source),
            (band_v_hbm, band_v), (band_c_hbm, band_c), (energy_hbm, energy), (occ_hbm, occ),
            (rho_re_hbm, dens.at[pl.ds(0, 32)]), (rho_im_hbm, dens.at[pl.ds(32, 32)]),
            (chi_prev, tile),
        ])
    ]
    for load in loads:
        load.start()
    barrier = pltpu.get_barrier_semaphore()
    for device in everyone:
        pl.semaphore_signal(barrier, inc=1, device_id=device, device_id_type=MESH)
    for load in loads[:2]:
        load.wait()

    scale16 = column(coulomb[...])
    src16 = source[...]
    both[my_k] = jnp.concatenate([src16, jnp.broadcast_to(scale16, (16, W))], axis=1)
    grid1[my_c, my_x, my_z] = scale16 * src16

    pl.semaphore_wait(barrier, len(everyone))

    send(both.at[my_k], both.at[my_k], both_sem.at[0], both_sem.at[1], at(k=other_k))

    def gather_start(grid, i):
        own = grid.at[my_c, my_x, my_z]
        for j, z in enumerate(z_peers):
            send(own, own, gz_send.at[i, j], g_recv.at[i, my_x, my_z], at(z=z))
        for j, x in enumerate(x_peers):
            send(own, own, gx_send.at[i, j, my_z], g_recv.at[i, my_x, my_z], at(x=x))

    def gather_z(grid, i):
        def relay(z):
            held = grid.at[my_c, my_x, z]
            arrive(held, gz_send.at[i, 0], g_recv.at[i, my_x, z])
            for j, x in enumerate(x_peers):
                remote(held, held, gx_send.at[i, j, z], g_recv.at[i, my_x, z], at(x=x)).start()

        for d in range(1, NZ):
            @pl.when(my_z + d < NZ)
            def _():
                relay(my_z + d)

            @pl.when(my_z - d >= 0)
            def _():
                relay(my_z - d)

        row = grid.at[my_c, my_x]
        send(row, row, gs_send.at[i, my_x], gs_recv.at[i, my_x], at(c=other_c))

    def gather_x(grid, i):
        for j in (0, NX - 2, 1) if NX == 4 else range(NX - 1):
            x = x_peers[j]
            for z in range(NZ):
                arrive(grid.at[my_c, x, z], gz_send.at[i, 0], g_recv.at[i, x, z])
            row = grid.at[my_c, x]
            send(row, row, gs_send.at[i, x], gs_recv.at[i, x], at(c=other_c))

    def gather_end(grid, i):
        for x in range(NX):
            arrive(grid.at[other_c, x], gs_send.at[i, 0], gs_recv.at[i, x])
        value = jnp.concatenate(
            [grid[c, x, z] for x in range(NX) for z in range(NZ) for c in range(NC)], axis=0
        )
        return split(value)

    def gather_close(grid, i):
        for j, x in enumerate(x_peers):
            for d in range(1, NZ):
                z = z_peers[d - 1]
                held = grid.at[my_c, my_x, z]
                remote(held, held, gx_send.at[i, j, z], g_recv.at[i, my_x, z], at(x=x)).wait_send()

    def project(v_re, v_im, i):
        stacked = jnp.concatenate(
            [jnp.concatenate([v_re, v_im], axis=1), jnp.concatenate([v_im, -v_re], axis=1)], axis=0
        )
        high, low = split(stacked)
        value = dot(pairs_t[...], jnp.concatenate([high, high, low], axis=0))
        count = n_pairs // NC // NX
        for c in range(NC):
            for x in range(NX):
                for t in range(n_tiles):
                    row = (c * NX + x) * count + (t // 2) * 8
                    lane = (t % 2) * W
                    part0[i, c, x, t] = value[row : row + 8, lane : lane + W]
        for x in x_order:
            send(part0.at[i, other_c, x], sib_in.at[i, x], sib_send.at[i, x], sib_recv.at[i, x], at(c=other_c))

    def reduce_x(i):
        for j, x in enumerate(x_order):
            arrive(sib_in.at[i, x], sib_send.at[i, x], sib_recv.at[i, x])
            part1[i, x] = part0[i, my_c, x] + sib_in[i, x]
            if j == NX - 1:
                continue
            send(part1.at[i, x], x_in.at[i, my_x], xr_send.at[i, j], xr_recv.at[i, my_x], at(x=x))

    def reduce_y(i):
        total = part1[i, my_x]
        for x in x_peers:
            arrive(x_in.at[i, x], xr_send.at[i, 0], xr_recv.at[i, x])
            total = total + x_in[i, x]
        part2[i] = total.reshape(part2.shape[1:])
        for j, y in enumerate(y_peers):
            send(part2.at[i, y], y_in.at[i, my_y], yr_send.at[i, j], yr_recv.at[i, my_y], at(y=y))

    def reduce_z(i):
        total = part2[i, my_y]
        for y in y_peers:
            arrive(y_in.at[i, y], yr_send.at[i, 0], yr_recv.at[i, y])
            total = total + y_in[i, y]
        z_all[i, my_k, my_z] = total
        own = z_all.at[i, my_k, my_z]
        for j, (z, k) in enumerate(ring):
            send(own, own, za_send.at[i, j], za_recv.at[i, my_k, my_z], at(z=z, k=k))

    def spread_y(i):
        for z, k in ring:
            arrive(z_all.at[i, k, z], za_send.at[i, 0], za_recv.at[i, k, z])
        for k in range(2):
            total = z_all[i, k, 0]
            for z in range(1, NZ):
                total = total + z_all[i, k, z]
            for t in range(per_y):
                full[i, my_c, my_x, my_y * per_y + t, k] = total[t]
        own = full.at[i, my_c, my_x, pl.ds(my_y * per_y, per_y)]
        for j, y in enumerate(y_peers):
            send(own, own, yg_send.at[i, j], yg_recv.at[i, my_y], at(y=y))

    def spread_x(i):
        for y in y_peers:
            arrive(full.at[i, my_c, my_x, pl.ds(y * per_y, per_y)], yg_send.at[i, 0], yg_recv.at[i, y])
        own = full.at[i, my_c, my_x]
        for j, x in enumerate(x_peers):
            send(own, own, xg_send.at[i, j], xg_recv.at[i, my_x], at(x=x))
        send(own, own, sg_send.at[i, my_x], sg_recv.at[i, my_x], at(c=other_c))

    def spread_core(i):
        for x in x_peers:
            held = full.at[i, my_c, x]
            arrive(held, xg_send.at[i, 0], xg_recv.at[i, x])
            send(held, held, sg_send.at[i, x], sg_recv.at[i, x], at(c=other_c))

    def expand(i):
        for x in range(NX):
            arrive(full.at[i, other_c, x], sg_send.at[i, 0], sg_recv.at[i, x])
        lanes = []
        for lane in range(2):
            lanes.append(jnp.concatenate(
                [full[i, c, x, t, k]
                 for k in range(2) for c in range(NC) for x in range(NX) for t in range(lane, n_tiles, 2)], axis=0
            ))
        high, low = split(jnp.concatenate(lanes, axis=1))
        left_hi, left_lo = split(jnp.concatenate([pairs_w[0], pairs_w[1]], axis=1))
        value = dot(left_hi, high) + dot(left_hi, low) + dot(left_lo, high)
        return jnp.concatenate(
            [value[:32, :W] - value[32:, W:], value[:32, W:] + value[32:, :W]], axis=1
        )

    def scatter_store(re, im, i):
        for y in range(ny):
            sums[i, y] = jnp.concatenate([re[y * 32 : y * 32 + 32], im[y * 32 : y * 32 + 32]], axis=1)

    def scatter_start(i):
        for j, y in enumerate(y_peers):
            send(sums.at[i, y], sums_in.at[i, my_y], rs_send.at[i, j], rs_recv.at[i, my_y], at(y=y))

    def scatter_end(i):
        total = sums[i, my_y]
        for y in y_peers:
            arrive(sums_in.at[i, y], rs_send.at[i, 0], rs_recv.at[i, y])
            total = total + sums_in[i, y]
        return total

    gather_start(grid1, 0)

    for load in loads[2:8]:
        load.wait()
    down = lax.broadcasted_iota(jnp.int32, (energy.shape[1], n_pairs), 0)
    in_v = down == band_v[...]
    in_c = down == band_c[...]
    e_col = column(energy[...])
    o_col = column(occ[...])

    def pick(match, table):
        return jnp.sum(jnp.where(match, table, 0.0), axis=0, keepdims=True)

    delta = pick(in_c, e_col) - pick(in_v, e_col)
    filling = pick(in_v, o_col) - pick(in_c, o_col)
    weight = filling * 2.0 * delta / (delta * delta + frequency * frequency)
    stacked_pairs = dens[...]
    high, low = split(stacked_pairs)
    high, low = high.astype(F32), low.astype(F32)
    pairs_t[...] = jnp.concatenate([high, low, high], axis=0).T.astype(BF16)
    pairs_w[my_k] = stacked_pairs * weight

    loads[8].wait()
    for part in range(2):
        for step in range(groups // 8):
            turned = tile[part, step * 8 : step * 8 + 8, 0].reshape(128, block).T
            high, low = split(turned)
            rows = pl.ds(part * block, block)
            lanes = pl.ds(step * 128, 128)
            wide_hi[rows, lanes] = high
            wide_lo[rows, lanes] = low

    gather_z(grid1, 0)
    arrive(both.at[other_k], both_sem.at[0], both_sem.at[1])
    held = both[...].reshape(32, 2 * W)
    src = held[:, :W]
    scale = held[:, W:]
    real_part = src
    imag_part = jnp.zeros_like(src)

    for i in range(ITERS):
        grid = grid1 if i == 0 else grid2
        v_re = scale * real_part
        v_im = scale * imag_part
        if i == 0:
            project(v_re, v_im, i)
            reduce_x(i)
            gather_x(grid, i)
            send(pairs_w.at[my_k], pairs_w.at[my_k], w_sem.at[0], w_sem.at[1], at(k=other_k))
            high, low = gather_end(grid, i)
            value = dot(wide_hi[...], jnp.concatenate([high, low], axis=1))
            value = value[:, :W] + value[:, W:] + dot(wide_lo[...], high)
            scatter_store(value[:block], value[block:], i)
            reduce_y(i)
            scatter_start(i)
            reduce_z(i)
        else:
            scaled[...] = jnp.concatenate([v_re, v_im], axis=1).reshape(scaled.shape)
            grid[my_c, my_x, my_z] = scaled[my_k]
            gather_start(grid, i)
            project(v_re, v_im, i)
            reduce_x(i)
            gather_z(grid, i)
            reduce_y(i)
            reduce_z(i)
            gather_x(grid, i)
            high, low = gather_end(grid, i)
            value = dot(wide_hi[...], high) + dot(wide_hi[...], low) + dot(wide_lo[...], high)
            scatter_store(value[:block, :W] - value[block:, W:], value[:block, W:] + value[block:, :W], i)
            scatter_start(i)
        spread_y(i)
        if i < ITERS - 1:
            halves[my_k] = scatter_end(i)
            send(halves.at[my_k], halves.at[my_k], h_sem.at[0, i], h_sem.at[1, i], at(k=other_k))
            spread_x(i)
            spread_core(i)
            arrive(halves.at[other_k], h_sem.at[0, i], h_sem.at[1, i])
            arrive(pairs_w.at[other_k], w_sem.at[0], w_sem.at[1])
            image = halves[0] + halves[1] - expand(i)
            real_part = real_part + damping * (src + scale * image[:, :W] - real_part)
            imag_part = imag_part + damping * (scale * image[:, W:] - imag_part)
            state[...] = jnp.concatenate([real_part, imag_part], axis=1).reshape(state.shape)
        else:
            last[...] = scatter_end(i).reshape(last.shape)
            send(last.at[other_k], last_in, h_sem.at[0, i], h_sem.at[1, i], at(k=other_k))
            spread_x(i)
            spread_core(i)
            for copy in sent:
                copy.wait_send()
            gather_close(grid1, 0)
            gather_close(grid2, 1)
            arrive(last_in, h_sem.at[0, i], h_sem.at[1, i])
            product[...] = expand(i).reshape(product.shape)
            image = scale16 * (last[my_k] + last_in[...] - product[my_k])
            mine = state[my_k]
            out[0] = mine[:, :W] + damping * (src16 + image[:, :W] - mine[:, :W])
            out[1] = mine[:, W:] + damping * (image[:, W:] - mine[:, W:])


def shards(ny, rho_re, rho_im, coulomb, chi_prev, source, band_v, band_c, energy, occ):
    n_pairs = rho_re.shape[1]
    groups, rows, block = chi_prev.shape[1], chi_prev.shape[3], chi_prev.shape[4]
    n_tiles = 2 * (n_pairs // NC // NX // 8)
    per_y = n_tiles // ny
    n = ITERS
    dma = pltpu.SemaphoreType.DMA
    vmem = pltpu.VMEM
    out = jax.ShapeDtypeStruct((2, rows, W), F32)
    in_vmem = pl.BlockSpec(memory_space=pltpu.VMEM)
    scratch = [
        vmem((64, n_pairs), F32), vmem((1, 16), F32), vmem((rows, W), F32),
        vmem((1, n_pairs), jnp.int32), vmem((1, n_pairs), jnp.int32),
        vmem((1, energy.shape[0]), F32), vmem((1, energy.shape[0]), F32), dma((9,)),
        vmem(chi_prev.shape, F32),
        vmem((2 * block, 16 * groups), BF16),
        vmem((2 * block, 16 * groups), BF16),
        vmem((n_pairs, 192), BF16),
        vmem((2, 64, n_pairs), F32),
        vmem((2, 16, 2 * W), F32),
        vmem((NC, NX, NZ, 16, W), F32),
        vmem((NC, NX, NZ, 16, 2 * W), F32),
        vmem((n, NC, NX, n_tiles, 8, W), F32),
        vmem((n, NX, n_tiles, 8, W), F32),
        vmem((n, NX, n_tiles, 8, W), F32),
        vmem((n, NX, n_tiles, 8, W), F32),
        vmem((n, ny, per_y, 8, W), F32),
        vmem((n, ny, per_y, 8, W), F32),
        vmem((n, 2, NZ, per_y, 8, W), F32),
        vmem((n, NC, NX, n_tiles, 2, 8, W), F32),
        vmem((n, ny, 32, 2 * W), F32),
        vmem((n, ny, 32, 2 * W), F32),
        vmem((2, 32, 2 * W), F32),
        vmem((2, 16, 2 * W), F32),
        vmem((2, 16, 2 * W), F32),
        vmem((2, 16, 2 * W), F32),
        vmem((16, 2 * W), F32),
        vmem((2, 16, 2 * W), F32),
        dma((2,)), dma((2,)),
        dma((n, NZ - 1)), dma((n, NX - 1, NZ)), dma((n, NX)), dma((n, NX, NZ)), dma((n, NX)),
        dma((n, NX)), dma((n, NX)), dma((n, NX - 1)), dma((n, NX)), dma((n, ny - 1)), dma((n, ny)),
        dma((n, 2 * NZ - 1)), dma((n, 2, NZ)), dma((n, ny - 1)), dma((n, ny)),
        dma((n, NX - 1)), dma((n, NX)), dma((n, NX)), dma((n, NX)),
        dma((n, ny - 1)), dma((n, ny)), dma((2, n)),
    ]
    result = pl.pallas_call(
        functools.partial(kernel, ny),
        out_shape=out,
        in_specs=[pl.BlockSpec(memory_space=pltpu.HBM)] * 9,
        out_specs=in_vmem,
        scratch_shapes=scratch,
        compiler_params=pltpu.CompilerParams(
            collective_id=0, has_side_effects=True, vmem_limit_bytes=48 * 1024 * 1024
        ),
        name="dyson",
    )(
        *[
            pltpu.with_memory_space_constraint(operand, pltpu.HBM)
            for operand in (
                rho_re, rho_im, coulomb.reshape(1, -1), chi_prev, source,
                band_v.reshape(1, -1), band_c.reshape(1, -1), energy.reshape(1, -1), occ.reshape(1, -1),
            )
        ]
    )
    return result[0], result[1]


def solution(mesh):
    placed = (
        P(("grp", "col"), "dev"),
        P(("grp", "col"), "dev"),
        P(("grp", "col", "dev")),
        P(None, None, "col", "dev", "grp"),
        P(("grp", "col", "dev"), None),
        P("dev"),
        P("dev"),
        P(),
        P(),
    )
    return jax.shard_map(
        functools.partial(shards, mesh.shape["col"]),
        mesh=mesh,
        in_specs=placed,
        out_specs=(P(("grp", "col", "dev"), None), P(("grp", "col", "dev"), None)),
        check_vma=False,
    )
```

```python
import functools

import jax
import jax.numpy as jnp
from jax import lax
from jax.experimental import pallas as pl
from jax.experimental.pallas import tpu as pltpu
from jax.sharding import PartitionSpec as P

ITERS = 2
NX = 4
NZ = 6
NC = 2
W = 128
frequency = 0.8
damping = 0.5
F32 = jnp.float32
BF16 = jnp.bfloat16
MESH = pl.DeviceIdType.MESH


def split(value):
    high = value.astype(BF16)
    low = (value - high.astype(F32)).astype(BF16)
    return high, low


def dot(left, right):
    return jnp.dot(left, right, preferred_element_type=F32)


def column(row):
    n = row.shape[1]
    down = lax.broadcasted_iota(jnp.int32, (n, n), 0)
    across = lax.broadcasted_iota(jnp.int32, (n, n), 1)
    return jnp.sum(jnp.where(down == across, row, 0.0), axis=1, keepdims=True)


def kernel(ny, rho_re_hbm, rho_im_hbm, coulomb_hbm, chi_prev, source_hbm, band_v_hbm, band_c_hbm, energy_hbm, occ_hbm,
           out,
           dens, coulomb, source, band_v, band_c, energy, occ, in_sem,
           tile, wide_hi, wide_lo, pairs_t, pairs_w, both, grid1, grid2,
           part0, sib_in, part1, x_in, part2, y_in, z_all, full, sums, sums_in, halves, scaled, state, last, last_in, product,
           both_sem, w_sem, gz_send, gx_send, gs_send, g_recv, gs_recv,
           sib_send, sib_recv, xr_send, xr_recv, yr_send, yr_recv, za_send, za_recv, yg_send, yg_recv,
           xg_send, xg_recv, sg_send, sg_recv, rs_send, rs_recv, h_sem):
    grp = lax.axis_index("grp")
    my_y = lax.axis_index("col")
    my_k = lax.axis_index("dev")
    my_c = lax.rem(grp, NC)
    my_z = lax.rem(lax.div(grp, NC), NZ)
    my_x = lax.div(grp, NC * NZ)
    other_c = 1 - my_c
    other_k = 1 - my_k
    groups = NX * NZ * NC
    n_pairs = dens.shape[1]
    n_tiles = full.shape[3]
    per_y = n_tiles // ny
    block = tile.shape[4]

    def at(x=None, y=None, z=None, c=None, k=None):
        x = my_x if x is None else x
        y = my_y if y is None else y
        z = my_z if z is None else z
        c = my_c if c is None else c
        k = my_k if k is None else k
        return ((x * NZ + z) * NC + c, y, k)

    x_peers = [lax.rem(my_x + d, NX) for d in sorted(range(1, NX), key=lambda d: -min(d, NX - d))]
    y_peers = [lax.rem(my_y + d, ny) for d in sorted(range(1, ny), key=lambda d: -min(d, ny - d))]
    x_order = x_peers + [my_x]
    z_peers = [lax.rem(my_z + d, NZ) for d in range(1, NZ)]
    ring = [(my_z, other_k)] + [(z, k) for z in z_peers for k in (other_k, my_k)]
    everyone = (
        [at(x=x) for x in x_peers]
        + [at(y=y) for y in y_peers]
        + [at(z=z) for z in z_peers]
        + [at(z=z, k=other_k) for z in z_peers]
        + [at(c=other_c), at(k=other_k)]
    )

    def remote(src, dst, send, recv, device):
        return pltpu.make_async_remote_copy(
            src_ref=src, dst_ref=dst, send_sem=send, recv_sem=recv, device_id=device, device_id_type=MESH
        )

    sent = []

    def send(src, dst, s, r, device):
        copy = remote(src, dst, s, r, device)
        copy.start()
        sent.append(copy)

    def arrive(dst, s, r):
        remote(dst, dst, s, r, at(c=other_c)).wait_recv()

    loads = [
        pltpu.make_async_copy(src, dst, in_sem.at[j])
        for j, (src, dst) in enumerate([
            (coulomb_hbm, coulomb), (source_hbm, source),
            (band_v_hbm, band_v), (band_c_hbm, band_c), (energy_hbm, energy), (occ_hbm, occ),
            (rho_re_hbm, dens.at[pl.ds(0, 32)]), (rho_im_hbm, dens.at[pl.ds(32, 32)]),
            (chi_prev, tile),
        ])
    ]
    for load in loads:
        load.start()
    barrier = pltpu.get_barrier_semaphore()
    for device in everyone:
        pl.semaphore_signal(barrier, inc=1, device_id=device, device_id_type=MESH)
    for load in loads[:2]:
        load.wait()

    scale16 = column(coulomb[...])
    src16 = source[...]
    both[my_k] = jnp.concatenate([src16, jnp.broadcast_to(scale16, (16, W))], axis=1)
    grid1[my_c, my_x, my_z] = scale16 * src16

    pl.semaphore_wait(barrier, len(everyone))

    send(both.at[my_k], both.at[my_k], both_sem.at[0], both_sem.at[1], at(k=other_k))

    def gather_start(grid, i):
        own = grid.at[my_c, my_x, my_z]
        for j, z in enumerate(z_peers):
            send(own, own, gz_send.at[i, j], g_recv.at[i, my_x, my_z], at(z=z))
        for j, x in enumerate(x_peers):
            send(own, own, gx_send.at[i, j, my_z], g_recv.at[i, my_x, my_z], at(x=x))

    def gather_z(grid, i):
        def relay(z):
            held = grid.at[my_c, my_x, z]
            arrive(held, gz_send.at[i, 0], g_recv.at[i, my_x, z])
            for j, x in enumerate(x_peers):
                remote(held, held, gx_send.at[i, j, z], g_recv.at[i, my_x, z], at(x=x)).start()

        for d in range(1, NZ):
            @pl.when(my_z + d < NZ)
            def _():
                relay(my_z + d)

            @pl.when(my_z - d >= 0)
            def _():
                relay(my_z - d)

        row = grid.at[my_c, my_x]
        send(row, row, gs_send.at[i, my_x], gs_recv.at[i, my_x], at(c=other_c))

    def gather_x(grid, i):
        for x in reversed(x_peers):
            for z in range(NZ):
                arrive(grid.at[my_c, x, z], gz_send.at[i, 0], g_recv.at[i, x, z])
            row = grid.at[my_c, x]
            send(row, row, gs_send.at[i, x], gs_recv.at[i, x], at(c=other_c))

    def gather_end(grid, i):
        for x in range(NX):
            arrive(grid.at[other_c, x], gs_send.at[i, 0], gs_recv.at[i, x])
        value = jnp.concatenate(
            [grid[c, x, z] for x in range(NX) for z in range(NZ) for c in range(NC)], axis=0
        )
        return split(value)

    def gather_close(grid, i):
        for j, x in enumerate(x_peers):
            for d in range(1, NZ):
                z = z_peers[d - 1]
                held = grid.at[my_c, my_x, z]
                remote(held, held, gx_send.at[i, j, z], g_recv.at[i, my_x, z], at(x=x)).wait_send()

    def project(v_re, v_im, i):
        stacked = jnp.concatenate(
            [jnp.concatenate([v_re, v_im], axis=1), jnp.concatenate([v_im, -v_re], axis=1)], axis=0
        )
        high, low = split(stacked)
        value = dot(pairs_t[...], jnp.concatenate([high, high, low], axis=0))
        count = n_pairs // NC // NX
        for c in range(NC):
            for x in range(NX):
                for t in range(n_tiles):
                    row = (c * NX + x) * count + (t // 2) * 8
                    lane = (t % 2) * W
                    part0[i, c, x, t] = value[row : row + 8, lane : lane + W]
        for x in x_order:
            send(part0.at[i, other_c, x], sib_in.at[i, x], sib_send.at[i, x], sib_recv.at[i, x], at(c=other_c))

    def reduce_x(i):
        for j, x in enumerate(x_order):
            arrive(sib_in.at[i, x], sib_send.at[i, x], sib_recv.at[i, x])
            part1[i, x] = part0[i, my_c, x] + sib_in[i, x]
            if j == NX - 1:
                continue
            send(part1.at[i, x], x_in.at[i, my_x], xr_send.at[i, j], xr_recv.at[i, my_x], at(x=x))

    def reduce_y(i):
        total = part1[i, my_x]
        for x in x_peers:
            arrive(x_in.at[i, x], xr_send.at[i, 0], xr_recv.at[i, x])
            total = total + x_in[i, x]
        part2[i] = total.reshape(part2.shape[1:])
        for j, y in enumerate(y_peers):
            send(part2.at[i, y], y_in.at[i, my_y], yr_send.at[i, j], yr_recv.at[i, my_y], at(y=y))

    def reduce_z(i):
        total = part2[i, my_y]
        for y in y_peers:
            arrive(y_in.at[i, y], yr_send.at[i, 0], yr_recv.at[i, y])
            total = total + y_in[i, y]
        z_all[i, my_k, my_z] = total
        own = z_all.at[i, my_k, my_z]
        for j, (z, k) in enumerate(ring):
            send(own, own, za_send.at[i, j], za_recv.at[i, my_k, my_z], at(z=z, k=k))

    def spread_y(i):
        for z, k in ring:
            arrive(z_all.at[i, k, z], za_send.at[i, 0], za_recv.at[i, k, z])
        for k in range(2):
            total = z_all[i, k, 0]
            for z in range(1, NZ):
                total = total + z_all[i, k, z]
            for t in range(per_y):
                full[i, my_c, my_x, my_y * per_y + t, k] = total[t]
        own = full.at[i, my_c, my_x, pl.ds(my_y * per_y, per_y)]
        for j, y in enumerate(y_peers):
            send(own, own, yg_send.at[i, j], yg_recv.at[i, my_y], at(y=y))

    def spread_x(i):
        for y in y_peers:
            arrive(full.at[i, my_c, my_x, pl.ds(y * per_y, per_y)], yg_send.at[i, 0], yg_recv.at[i, y])
        own = full.at[i, my_c, my_x]
        for j, x in enumerate(x_peers):
            send(own, own, xg_send.at[i, j], xg_recv.at[i, my_x], at(x=x))
        send(own, own, sg_send.at[i, my_x], sg_recv.at[i, my_x], at(c=other_c))

    def spread_core(i):
        for x in reversed(x_peers):
            held = full.at[i, my_c, x]
            arrive(held, xg_send.at[i, 0], xg_recv.at[i, x])
            send(held, held, sg_send.at[i, x], sg_recv.at[i, x], at(c=other_c))

    def expand(i):
        for x in range(NX):
            arrive(full.at[i, other_c, x], sg_send.at[i, 0], sg_recv.at[i, x])
        lanes = []
        for lane in range(2):
            lanes.append(jnp.concatenate(
                [full[i, c, x, t, k]
                 for k in range(2) for c in range(NC) for x in range(NX) for t in range(lane, n_tiles, 2)], axis=0
            ))
        high, low = split(jnp.concatenate(lanes, axis=1))
        left_hi, left_lo = split(jnp.concatenate([pairs_w[0], pairs_w[1]], axis=1))
        value = dot(left_hi, high) + dot(left_hi, low) + dot(left_lo, high)
        return jnp.concatenate(
            [value[:32, :W] - value[32:, W:], value[:32, W:] + value[32:, :W]], axis=1
        )

    def scatter_store(re, im, i):
        for y in range(ny):
            sums[i, y] = jnp.concatenate([re[y * 32 : y * 32 + 32], im[y * 32 : y * 32 + 32]], axis=1)

    def scatter_start(i):
        for j, y in enumerate(y_peers):
            send(sums.at[i, y], sums_in.at[i, my_y], rs_send.at[i, j], rs_recv.at[i, my_y], at(y=y))

    def scatter_end(i):
        total = sums[i, my_y]
        for y in y_peers:
            arrive(sums_in.at[i, y], rs_send.at[i, 0], rs_recv.at[i, y])
            total = total + sums_in[i, y]
        return total

    gather_start(grid1, 0)

    for load in loads[2:8]:
        load.wait()
    down = lax.broadcasted_iota(jnp.int32, (energy.shape[1], n_pairs), 0)
    in_v = down == band_v[...]
    in_c = down == band_c[...]
    e_col = column(energy[...])
    o_col = column(occ[...])

    def pick(match, table):
        return jnp.sum(jnp.where(match, table, 0.0), axis=0, keepdims=True)

    delta = pick(in_c, e_col) - pick(in_v, e_col)
    filling = pick(in_v, o_col) - pick(in_c, o_col)
    weight = filling * 2.0 * delta / (delta * delta + frequency * frequency)
    stacked_pairs = dens[...]
    high, low = split(stacked_pairs)
    high, low = high.astype(F32), low.astype(F32)
    pairs_t[...] = jnp.concatenate([high, low, high], axis=0).T.astype(BF16)
    pairs_w[my_k] = stacked_pairs * weight

    loads[8].wait()
    for part in range(2):
        for step in range(groups // 8):
            turned = tile[part, step * 8 : step * 8 + 8, 0].reshape(128, block).T
            high, low = split(turned)
            rows = pl.ds(part * block, block)
            lanes = pl.ds(step * 128, 128)
            wide_hi[rows, lanes] = high
            wide_lo[rows, lanes] = low

    gather_z(grid1, 0)
    arrive(both.at[other_k], both_sem.at[0], both_sem.at[1])
    held = both[...].reshape(32, 2 * W)
    src = held[:, :W]
    scale = held[:, W:]
    real_part = src
    imag_part = jnp.zeros_like(src)

    for i in range(ITERS):
        grid = grid1 if i == 0 else grid2
        v_re = scale * real_part
        v_im = scale * imag_part
        if i == 0:
            project(v_re, v_im, i)
            reduce_x(i)
            gather_x(grid, i)
            send(pairs_w.at[my_k], pairs_w.at[my_k], w_sem.at[0], w_sem.at[1], at(k=other_k))
            high, low = gather_end(grid, i)
            value = dot(wide_hi[...], jnp.concatenate([high, low], axis=1))
            value = value[:, :W] + value[:, W:] + dot(wide_lo[...], high)
            scatter_store(value[:block], value[block:], i)
            reduce_y(i)
            scatter_start(i)
            reduce_z(i)
        else:
            scaled[...] = jnp.concatenate([v_re, v_im], axis=1).reshape(scaled.shape)
            grid[my_c, my_x, my_z] = scaled[my_k]
            gather_start(grid, i)
            project(v_re, v_im, i)
            reduce_x(i)
            gather_z(grid, i)
            reduce_y(i)
            reduce_z(i)
            gather_x(grid, i)
            high, low = gather_end(grid, i)
            value = dot(wide_hi[...], high) + dot(wide_hi[...], low) + dot(wide_lo[...], high)
            scatter_store(value[:block, :W] - value[block:, W:], value[:block, W:] + value[block:, :W], i)
            scatter_start(i)
        spread_y(i)
        if i < ITERS - 1:
            halves[my_k] = scatter_end(i)
            send(halves.at[my_k], halves.at[my_k], h_sem.at[0, i], h_sem.at[1, i], at(k=other_k))
            spread_x(i)
            spread_core(i)
            arrive(halves.at[other_k], h_sem.at[0, i], h_sem.at[1, i])
            arrive(pairs_w.at[other_k], w_sem.at[0], w_sem.at[1])
            image = halves[0] + halves[1] - expand(i)
            real_part = real_part + damping * (src + scale * image[:, :W] - real_part)
            imag_part = imag_part + damping * (scale * image[:, W:] - imag_part)
            state[...] = jnp.concatenate([real_part, imag_part], axis=1).reshape(state.shape)
        else:
            last[...] = scatter_end(i).reshape(last.shape)
            send(last.at[other_k], last_in, h_sem.at[0, i], h_sem.at[1, i], at(k=other_k))
            spread_x(i)
            spread_core(i)
            for copy in sent:
                copy.wait_send()
            gather_close(grid1, 0)
            gather_close(grid2, 1)
            arrive(last_in, h_sem.at[0, i], h_sem.at[1, i])
            product[...] = expand(i).reshape(product.shape)
            image = scale16 * (last[my_k] + last_in[...] - product[my_k])
            mine = state[my_k]
            out[0] = mine[:, :W] + damping * (src16 + image[:, :W] - mine[:, :W])
            out[1] = mine[:, W:] + damping * (image[:, W:] - mine[:, W:])


def shards(ny, rho_re, rho_im, coulomb, chi_prev, source, band_v, band_c, energy, occ):
    n_pairs = rho_re.shape[1]
    groups, rows, block = chi_prev.shape[1], chi_prev.shape[3], chi_prev.shape[4]
    n_tiles = 2 * (n_pairs // NC // NX // 8)
    per_y = n_tiles // ny
    n = ITERS
    dma = pltpu.SemaphoreType.DMA
    vmem = pltpu.VMEM
    out = jax.ShapeDtypeStruct((2, rows, W), F32)
    in_vmem = pl.BlockSpec(memory_space=pltpu.VMEM)
    scratch = [
        vmem((64, n_pairs), F32), vmem((1, 16), F32), vmem((rows, W), F32),
        vmem((1, n_pairs), jnp.int32), vmem((1, n_pairs), jnp.int32),
        vmem((1, energy.shape[0]), F32), vmem((1, energy.shape[0]), F32), dma((9,)),
        vmem(chi_prev.shape, F32),
        vmem((2 * block, 16 * groups), BF16),
        vmem((2 * block, 16 * groups), BF16),
        vmem((n_pairs, 192), BF16),
        vmem((2, 64, n_pairs), F32),
        vmem((2, 16, 2 * W), F32),
        vmem((NC, NX, NZ, 16, W), F32),
        vmem((NC, NX, NZ, 16, 2 * W), F32),
        vmem((n, NC, NX, n_tiles, 8, W), F32),
        vmem((n, NX, n_tiles, 8, W), F32),
        vmem((n, NX, n_tiles, 8, W), F32),
        vmem((n, NX, n_tiles, 8, W), F32),
        vmem((n, ny, per_y, 8, W), F32),
        vmem((n, ny, per_y, 8, W), F32),
        vmem((n, 2, NZ, per_y, 8, W), F32),
        vmem((n, NC, NX, n_tiles, 2, 8, W), F32),
        vmem((n, ny, 32, 2 * W), F32),
        vmem((n, ny, 32, 2 * W), F32),
        vmem((2, 32, 2 * W), F32),
        vmem((2, 16, 2 * W), F32),
        vmem((2, 16, 2 * W), F32),
        vmem((2, 16, 2 * W), F32),
        vmem((16, 2 * W), F32),
        vmem((2, 16, 2 * W), F32),
        dma((2,)), dma((2,)),
        dma((n, NZ - 1)), dma((n, NX - 1, NZ)), dma((n, NX)), dma((n, NX, NZ)), dma((n, NX)),
        dma((n, NX)), dma((n, NX)), dma((n, NX - 1)), dma((n, NX)), dma((n, ny - 1)), dma((n, ny)),
        dma((n, 2 * NZ - 1)), dma((n, 2, NZ)), dma((n, ny - 1)), dma((n, ny)),
        dma((n, NX - 1)), dma((n, NX)), dma((n, NX)), dma((n, NX)),
        dma((n, ny - 1)), dma((n, ny)), dma((2, n)),
    ]
    result = pl.pallas_call(
        functools.partial(kernel, ny),
        out_shape=out,
        in_specs=[pl.BlockSpec(memory_space=pltpu.HBM)] * 9,
        out_specs=in_vmem,
        scratch_shapes=scratch,
        compiler_params=pltpu.CompilerParams(
            collective_id=0, has_side_effects=True, vmem_limit_bytes=48 * 1024 * 1024
        ),
        name="dyson",
    )(
        *[
            pltpu.with_memory_space_constraint(operand, pltpu.HBM)
            for operand in (
                rho_re, rho_im, coulomb.reshape(1, -1), chi_prev, source,
                band_v.reshape(1, -1), band_c.reshape(1, -1), energy.reshape(1, -1), occ.reshape(1, -1),
            )
        ]
    )
    return result[0], result[1]


def solution(mesh):
    placed = (
        P(("grp", "col"), "dev"),
        P(("grp", "col"), "dev"),
        P(("grp", "col", "dev")),
        P(None, None, "col", "dev", "grp"),
        P(("grp", "col", "dev"), None),
        P("dev"),
        P("dev"),
        P(),
        P(),
    )
    return jax.shard_map(
        functools.partial(shards, mesh.shape["col"]),
        mesh=mesh,
        in_specs=placed,
        out_specs=(P(("grp", "col", "dev"), None), P(("grp", "col", "dev"), None)),
        check_vma=False,
    )
```
